32 devices in a mesh: grp: 2 (over y), row: 4 (over z), col: 2 (over core), chan: 2 (over x).
Axes of the slice: x: 2, y: 2, z: 4, core: 2. Of those that a mesh axis runs over, the one named last changes fastest.
Arguments:
- theta: bfloat16 [2048, 16, 1024], P(('grp', 'row'), None, ('col', 'chan')), parts along dimension 0, may hold values from -6 to 6
- left_env: bfloat16 [2048, 12, 1024], P(('grp', 'row')), parts along dimension 0, may hold values from -0.25 to 0.25
- right_env: bfloat16 [2048, 12, 1024], P('grp', None, ('col', 'chan')), parts along dimension 0, may hold values from -0.078125 to 0.078125
- mpo_left: float32 [12, 12, 4, 4], replicated, may hold values from -0.875 to 0.875
- mpo_right: float32 [12, 12, 4, 4], replicated, may hold values from -0.875 to 0.875
Outputs:
- residual: bfloat16 [2048, 16384], P(('grp', 'col', 'chan'), 'row'), parts along dimension 0
- hvp: bfloat16 [2048, 16, 1024], P(('grp', 'row'), None, ('col', 'chan')), parts along dimension 0
The draws below stay inside these ranges and needn't reach their ends.
There are 2 independent parts, one for each index of `grp`. The reference program is written for one: setup_inputs(seed, part) draws one part's arguments, and reference() takes and returns one part's arrays. A program takes and returns all parts, laid end to end along the dimension named above; an argument that names none is the same for every part. Nothing has to cross between parts.
All inputs are finite; a program needn't handle non-finite values.
Results may differ from the reference program's by a relative error of at most 0.025.
Values may be sent and summed in bfloat16 or wider, within the bound.
A program may use at most 128 MiB of HBM per device.

```python
import jax
import jax.numpy as jnp
from jax import lax

D = 1024
W = 12
PHYS = 4
S = 16


def with_spikes(values, rng, source, target, shards_of, factor):
    owner, partner = [(jnp.arange(values.shape[dim]) // (values.shape[dim] // shards_of)).reshape([-1 if axis == dim else 1 for axis in range(values.ndim)]) for dim in (source, target)]
    chosen = jax.random.permutation(rng, shards_of)[partner]
    strong = (owner == chosen) | (owner == (partner + shards_of // 2) % shards_of)
    return jnp.where(strong, factor * values, values)


def block_scale(key, extent, shards, least, top_value):
    gain, own = 1.0, jax.random.fold_in(key, 6)
    for dim, parts in shards:
        draws = jnp.exp(jax.random.uniform(jax.random.fold_in(own, dim), (parts,), jnp.float32, least / len(shards), top_value / len(shards)))
        gain = gain * jnp.repeat(draws, extent[dim] // parts).reshape([-1 if axis == dim else 1 for axis in range(len(extent))])
    return gain


def normal_values(stream_key, shape, scale, most, cuts=(), kind=jnp.bfloat16):
    entries = jax.random.normal(stream_key, shape, jnp.float32) * scale
    if len(cuts) > 0:
        entries = block_scale(stream_key, shape, cuts, -0.22, 0.18) * entries
    return jnp.clip(entries, min=-most, max=most).astype(kind)


def gaussian_with(own_key, extent, spread, bound, shards, heavy, held_as=jnp.bfloat16):
    result = spread * jax.random.normal(own_key, extent, jnp.float32)
    if shards:
        result = result * block_scale(own_key, extent, shards, -0.22, 0.18)
    return jnp.clip(with_spikes(result, jax.random.fold_in(own_key, 3), *heavy), -bound, bound).astype(held_as)


def setup_inputs(seed: int = 0, part: int = 0) -> dict:
    arg_keys = jax.random.split(jax.random.key(seed), 6)
    part_keys = jax.random.split(jax.random.fold_in(arg_keys[5], part), 6)
    return {
        "theta": normal_values(part_keys[0], (D, S, D), 1.0, 6.0, ((0, 4), (2, 4))),
        "left_env": gaussian_with(part_keys[1], (D, W, D), D ** -0.5, 0.25, ((0, 4),), (0, 2, 4, 2.0)),
        "right_env": gaussian_with(part_keys[2], (D, W, D), (W * D) ** -0.5, 0.078125, ((2, 4),), (2, 0, 4, 2.0)),
        "mpo_left": normal_values(arg_keys[3], (W, W, PHYS, PHYS), (W * PHYS) ** -0.5, 0.875, (), jnp.float32),
        "mpo_right": normal_values(arg_keys[4], (W, W, PHYS, PHYS), (W * PHYS) ** -0.5, 0.875, (), jnp.float32),
    }


def mpo_product(mpo_left, mpo_right):
    paired = jnp.einsum('wuxs,uvyt->wstxyv', mpo_left, mpo_right, precision=lax.Precision.HIGHEST)
    return paired.reshape(W * PHYS * PHYS, PHYS * PHYS * W).astype(jnp.bfloat16)


def rounded(values):
    return lax.optimization_barrier(values.astype(jnp.bfloat16)).astype(jnp.float32)


def reference(theta, left_env, right_env, mpo_left, mpo_right):
    mpo_pair = mpo_product(mpo_left, mpo_right).astype(jnp.float32)
    theta_wide = theta.astype(jnp.float32)
    right_wide = right_env.astype(jnp.float32)
    stride = min(64, D)
    blocks = D // stride

    def step(total, index):
        begin = (index * stride).astype(jnp.int32)
        left_block = lax.dynamic_slice_in_dim(left_env, begin, stride, 0).astype(jnp.float32)
        section_one = rounded(jnp.einsum('awk,ksb->awsb', left_block, theta_wide))
        section_three = rounded(jnp.einsum('pq,apb->aqb', mpo_pair, section_one.reshape(stride, W * S, D)))
        section_three = section_three.reshape(stride, S, W, D)
        partial_res = jnp.einsum('kvb,asvb->kas', right_wide, section_three).reshape(D, stride * S)
        resid_block = partial_res.astype(jnp.bfloat16)
        back_one = rounded(jnp.einsum('kp,kvb->pvb', rounded(partial_res), right_wide))
        back_one = back_one.reshape(stride, S * W, D)
        back_two = rounded(jnp.einsum('pq,aqb->apb', mpo_pair, back_one)).reshape(stride, W, S, D)
        total = total + jnp.einsum('awk,awsb->ksb', left_block, back_two)
        return total, resid_block

    total, resid_blocks = lax.scan(step, jnp.zeros((D, S, D), jnp.float32), jnp.arange(blocks, dtype=jnp.int32))
    residual = jnp.transpose(resid_blocks, (1, 0, 2)).reshape(D, D * S)
    return residual, total.astype(jnp.bfloat16)
```

```python
import functools

import jax
import jax.numpy as jnp
from jax import lax
from jax.experimental import pallas as pl
from jax.experimental.pallas import tpu as pltpu
from jax.sharding import PartitionSpec as P

PAD = 16
AHEAD = 3
LIMIT = 56 * 1024 * 1024
MESH = pl.DeviceIdType.MESH


def cost(flops, size):
    return pl.CostEstimate(flops=int(flops), bytes_accessed=int(size), transcendentals=0)


def dot(lhs, rhs):
    return jnp.dot(lhs, rhs, preferred_element_type=jnp.float32)


def pair_dot(lhs, first, second):
    return dot(lhs, jnp.concatenate([first, second], axis=1)).astype(jnp.bfloat16)


def greet_row():
    size = lax.axis_size("row")
    barrier = pltpu.get_barrier_semaphore()
    for step in range(1, size):
        peer = lax.rem(lax.axis_index("row") + step, size)
        pl.semaphore_signal(barrier, inc=1, device_id={"row": peer}, device_id_type=MESH)
    pl.semaphore_wait(barrier, size - 1)


def remote(source, target, send_sem, recv_sem, row):
    return pltpu.make_async_remote_copy(
        src_ref=source,
        dst_ref=target,
        send_sem=send_sem,
        recv_sem=recv_sem,
        device_id={"row": row},
        device_id_type=MESH,
    )


GATHER_SENDS = {0: (1, 2), 1: (2, 0, 3), 2: (1, 3, 0), 3: (2, 1)}
GATHER_HANDS = {1: (3, 0), 2: (0, 3)}


def forward_kernel(
    pieces, theta_ref, left_hbm, mpo_ref, right_hbm, out_ref,
    gathered, left_ref, right_ref, held, three, total, stage, sent, got, local, outs,
):
    width = theta_ref.shape[1]
    tile, channels, pairs, lanes = held.shape
    parts, count, rows, _ = out_ref.shape
    step = tile * pairs
    depth = tile * PAD
    me = lax.axis_index("row")
    loads = [
        pltpu.make_async_copy(left_hbm, left_ref, local.at[0]),
        pltpu.make_async_copy(right_hbm, right_ref, local.at[1]),
    ]
    for item in loads:
        item.start()

    def at(piece):
        return pl.ds(pl.multiple_of(piece * step, step), step)

    def block(piece, origin):
        return gathered.at[at(piece), origin * width : (origin + 1) * width]

    def send(piece, origin, slot, row, source=None):
        source = theta_ref.at[at(piece), :] if source is None else source
        sems = sent.at[slot, piece], got.at[origin, piece]
        return remote(source, block(piece, origin), *sems, row)

    def arrival(piece, origin):
        return send(piece, origin, 0, me)

    greet_row()
    for r, rows_to in GATHER_SENDS.items():

        @pl.when(me == r)
        def _(r=r, rows_to=rows_to):
            for piece in range(min(AHEAD, pieces)):
                for slot, row in enumerate(rows_to):
                    send(piece, r, slot, row).start()
            mine = pltpu.make_async_copy(
                theta_ref, gathered.at[:, r * width : (r + 1) * width], local.at[2]
            )
            mine.start()
            mine.wait()

    def clear(x, carry):
        total[x] = jnp.zeros(total.shape[1:], total.dtype)
        return carry

    lax.fori_loop(0, total.shape[0], clear, 0)
    for item in loads:
        item.wait()

    def output(x, slot):
        return pltpu.make_async_copy(
            stage.at[slot], out_ref.at[:, pl.ds(2 * x, 2)], outs.at[slot]
        )

    def body(piece, carry):
        for r, rows_to in GATHER_SENDS.items():

            @pl.when(me == r)
            def _(r=r, rows_to=rows_to):
                late = [origin for origin in range(4) if origin != r]
                if r in GATHER_HANDS:
                    origin, row = GATHER_HANDS[r]
                    arrival(piece, origin).wait_recv()
                    send(piece, origin, len(rows_to), row, block(piece, origin)).start()
                    late.remove(origin)
                for origin in late:
                    arrival(piece, origin).wait_recv()

                @pl.when(piece + AHEAD < pieces)
                def _():
                    for slot, row in enumerate(rows_to):
                        send(piece + AHEAD, r, slot, row).start()

        def one(w, carry):
            where = pl.ds(pl.multiple_of(2 * w * lanes, 2 * lanes), 2 * lanes)
            part = lax.dot_general(
                gathered[at(piece), :],
                left_ref[where, :],
                (((1,), (1,)), ((), ())),
                preferred_element_type=jnp.float32,
            ).astype(jnp.bfloat16)
            held[:, 2 * w] = part[:, :lanes].reshape(tile, pairs, lanes)
            held[:, 2 * w + 1] = part[:, lanes:].reshape(tile, pairs, lanes)
            return carry

        lax.fori_loop(0, channels // 2, one, 0, unroll=2)

        def two(b, carry):
            first = held[2 * b].reshape(channels * pairs, lanes)
            second = held[2 * b + 1].reshape(channels * pairs, lanes)
            part = pair_dot(mpo_ref[...], first, second)
            three[:, 2 * b] = part[:, :lanes].reshape(pairs, PAD, lanes)
            three[:, 2 * b + 1] = part[:, lanes:].reshape(pairs, PAD, lanes)
            return carry

        lax.fori_loop(0, tile // 2, two, 0, unroll=4)

        def term(x):
            first, second = three[2 * x].reshape(depth, lanes), three[2 * x + 1].reshape(depth, lanes)
            where = pl.ds(pl.multiple_of(piece * depth, depth), depth)
            return total[x] + dot(right_ref[:, where], jnp.concatenate([first, second], axis=1))

        @pl.when(piece < pieces - 1)
        def _():
            def add(x, carry):
                total[x] = term(x)
                return carry

            lax.fori_loop(0, count // 2, add, 0)

        @pl.when(piece == pieces - 1)
        def _():
            def add(x, carry):
                slot = lax.rem(x, 2)

                @pl.when(x >= 2)
                def _():
                    output(x - 2, slot).wait()

                value = term(x).astype(out_ref.dtype)
                for j in range(2):
                    half = value[:, j * lanes : (j + 1) * lanes]
                    stage[slot, :, j] = half.reshape(parts, rows, lanes)
                output(x, slot).start()
                return carry

            lax.fori_loop(0, count // 2, add, 0)
            for x in range(count // 2 - 2, count // 2):
                output(x, x % 2).wait()

        return carry

    lax.fori_loop(0, pieces, body, 0)
    for r, rows_to in GATHER_SENDS.items():

        @pl.when(me == r)
        def _(r=r, rows_to=rows_to):
            def finish(piece, carry):
                for slot, row in enumerate(rows_to):
                    send(piece, r, slot, row).wait_send()
                if r in GATHER_HANDS:
                    origin, row = GATHER_HANDS[r]
                    send(piece, origin, len(rows_to), row, block(piece, origin)).wait_send()
                return carry

            lax.fori_loop(0, pieces, finish, 0)


def forward(theta, left, mpo, right, pairs, tile, parts):
    steps, width = theta.shape
    channels, depth = left.shape[0] // width, left.shape[1]
    lanes = width
    bonds = steps // pairs
    pieces = bonds // tile
    rows = right.shape[0]
    flops = 2 * steps * left.size + 2 * bonds * mpo.size * lanes
    flops += 2 * rows * bonds * PAD * pairs * lanes
    size = 2 * (theta.size + left.size + right.size) + 2 * rows * pairs * lanes
    far = pl.BlockSpec(memory_space=pl.ANY)
    return pl.pallas_call(
        functools.partial(forward_kernel, pieces),
        out_shape=jax.ShapeDtypeStruct((parts, pairs, rows // parts, lanes), jnp.bfloat16),
        in_specs=[far, far, pl.BlockSpec(memory_space=pltpu.VMEM), far],
        out_specs=far,
        scratch_shapes=[
            pltpu.VMEM((steps, depth), jnp.bfloat16),
            pltpu.VMEM(left.shape, jnp.bfloat16),
            pltpu.VMEM(right.shape, jnp.bfloat16),
            pltpu.VMEM((tile, channels, pairs, lanes), jnp.bfloat16),
            pltpu.VMEM((pairs, tile, PAD, lanes), jnp.bfloat16),
            pltpu.VMEM((pairs // 2, rows, 2 * lanes), jnp.float32),
            pltpu.VMEM((2, parts, 2, rows // parts, lanes), jnp.bfloat16),
            pltpu.SemaphoreType.DMA((4, pieces)),
            pltpu.SemaphoreType.DMA((4, pieces)),
            pltpu.SemaphoreType.DMA((3,)),
            pltpu.SemaphoreType.DMA((2,)),
        ],
        compiler_params=pltpu.CompilerParams(
            collective_id=1, has_side_effects=True, vmem_limit_bytes=LIMIT
        ),
        cost_estimate=cost(flops, size),
    )(theta, left, mpo, right)


def exchange_kernel(pieces, term, full, near, mine, far, sent, got):
    col, chan = lax.axis_index("col"), lax.axis_index("chan")
    chans, count, rows, lanes = mine.shape
    group = count // pieces
    core, chip = {"col": 1 - col}, {"chan": 1 - chan}
    barrier = pltpu.get_barrier_semaphore()
    for peer in (core, chip):
        pl.semaphore_signal(barrier, inc=1, device_id=peer, device_id_type=MESH)
    pl.semaphore_wait(barrier, 2)

    def copy(kind, j, source, target, peer):
        return pltpu.make_async_remote_copy(
            src_ref=source,
            dst_ref=target,
            send_sem=sent.at[kind, j],
            recv_sem=got.at[kind, j],
            device_id=peer,
            device_id_type=MESH,
        )

    spans = [pl.ds(j * group, group) for j in range(pieces)]
    firsts = [
        copy(0, j, term.at[1 - col, :, spans[j]], near.at[:, spans[j]], core) for j in range(pieces)
    ]
    seconds = [copy(1, j, mine.at[:, spans[j]], far.at[:, spans[j]], chip) for j in range(pieces)]
    block = pl.ds(col * chans, chans)
    thirds = [
        copy(2, j, full.at[block, spans[j]], full.at[block, spans[j]], core) for j in range(pieces)
    ]
    for item in firsts:
        item.start()
    for j in range(pieces):
        firsts[j].wait_recv()

        def first(x, carry):
            for q in range(chans):
                value = term[col, q, x].astype(jnp.float32) + near[q, x].astype(jnp.float32)
                mine[q, x] = value.astype(jnp.bfloat16)
            return carry

        lax.fori_loop(j * group, (j + 1) * group, first, 0)
        seconds[j].start()
    for j in range(pieces):
        seconds[j].wait_recv()

        def second(x, carry):
            for q in range(chans):
                value = mine[q, x].astype(jnp.float32) + far[q, x].astype(jnp.float32)
                full[col * chans + q, x] = value.astype(jnp.bfloat16)
            return carry

        lax.fori_loop(j * group, (j + 1) * group, second, 0)
        thirds[j].start()
    for j in range(pieces):
        thirds[j].wait_recv()
    for item in firsts + seconds + thirds:
        item.wait_send()


def exchange(term):
    cols, chans, count, rows, lanes = term.shape
    pieces = 8
    half = pltpu.VMEM((chans, count, rows, lanes), jnp.bfloat16)
    return pl.pallas_call(
        functools.partial(exchange_kernel, pieces),
        out_shape=jax.ShapeDtypeStruct((cols * chans, count, rows, lanes), jnp.bfloat16),
        in_specs=[pl.BlockSpec(memory_space=pltpu.VMEM)],
        out_specs=pl.BlockSpec(memory_space=pltpu.VMEM),
        scratch_shapes=[half, half, half]
        + [pltpu.SemaphoreType.DMA((3, pieces)), pltpu.SemaphoreType.DMA((3, pieces))],
        compiler_params=pltpu.CompilerParams(
            collective_id=0, has_side_effects=True, vmem_limit_bytes=LIMIT
        ),
        cost_estimate=cost(0, 4 * term.size),
    )(term)


SCATTER_SENDS = {
    0: ((1, 3), (1, 1), (2, 2)),
    1: ((2, 2), (0, 0)),
    2: ((1, 1), (3, 3)),
    3: ((2, 0), (2, 2), (1, 1)),
}
SCATTER_HANDS = {1: 3, 2: 0}
SCATTER_FROM = {0: (1, 2), 1: (0, 2, 3), 2: (3, 1, 0), 3: (2, 1)}


def backward_kernel(
    pieces, right_hbm, res_hbm, mpo_ref, left_hbm, out_ref,
    right_ref, res_ref, left_ref, held, lhs, made, come, sent, got, local, loads,
):
    tile, _, _, lanes = held.shape
    channels = lhs.shape[1] // lanes
    pairs = lhs.shape[0] // tile
    parts, count, rows, _ = res_ref.shape
    width = out_ref.shape[1]
    blocks = made.shape[0]
    step = tile * pairs
    depth = tile * PAD
    me = lax.axis_index("row")

    def load(piece, slot):
        where = pl.ds(pl.multiple_of(piece * depth, depth), depth)
        return pltpu.make_async_copy(right_hbm.at[where, :], right_ref.at[slot], loads.at[slot])

    load(0, 0).start()
    wholes = [
        pltpu.make_async_copy(res_hbm, res_ref, local.at[0]),
        pltpu.make_async_copy(left_hbm, left_ref, local.at[1]),
    ]
    for item in wholes:
        item.start()
    greet_row()

    def at(piece):
        return pl.ds(pl.multiple_of(piece * step, step), step)

    def send(piece, r, slot, row, owner):
        place = r if row == owner else row
        target = come.at[place, at(piece), :]
        sems = sent.at[slot, piece], got.at[place, piece]
        return remote(made.at[owner, at(piece), :], target, *sems, row)

    def arrival(piece, place):
        target = come.at[place, at(piece), :]
        return remote(target, target, sent.at[0, piece], got.at[place, piece], me)

    def hand(piece):
        for r, owner in SCATTER_HANDS.items():

            @pl.when(me == r)
            def _(r=r, owner=owner):
                arrival(piece, r).wait_recv()
                value = made[owner, at(piece), :].astype(jnp.float32)
                value = value + come[r, at(piece), :].astype(jnp.float32)
                made[owner, at(piece), :] = value.astype(jnp.bfloat16)
                send(piece, r, len(SCATTER_SENDS[r]), owner, owner).start()

    def finish(piece):
        for r, origins in SCATTER_FROM.items():

            @pl.when(me == r)
            def _(r=r, origins=origins):
                for place in origins:
                    arrival(piece, place).wait_recv()
                value = made[r, at(piece), :].astype(jnp.float32)
                for place in origins:
                    value = value + come[place, at(piece), :].astype(jnp.float32)
                out_ref[at(piece), :] = value.astype(jnp.bfloat16)

    for item in wholes:
        item.wait()

    def body(piece, carry):
        now = lax.rem(piece, 2)
        load(piece, now).wait()

        @pl.when(piece + 1 < pieces)
        def _():
            load(piece + 1, 1 - now).start()

        def five(x, carry):
            first = res_ref[:, 2 * x].reshape(parts * rows, lanes)
            second = res_ref[:, 2 * x + 1].reshape(parts * rows, lanes)
            part = pair_dot(right_ref[now], first, second)
            held[:, 2 * x] = part[:, :lanes].reshape(tile, PAD, lanes)
            held[:, 2 * x + 1] = part[:, lanes:].reshape(tile, PAD, lanes)
            return carry

        lax.fori_loop(0, count // 2, five, 0, unroll=2)

        def six(b, carry):
            first = held[2 * b].reshape(count * PAD, lanes)
            second = held[2 * b + 1].reshape(count * PAD, lanes)
            part = pair_dot(mpo_ref[...], first, second)
            for j in range(2):
                where = pl.ds(pl.multiple_of((2 * b + j) * pairs, pairs), pairs)
                half = part[:, j * lanes : (j + 1) * lanes]
                for w in range(channels):
                    lhs[where, w * lanes : (w + 1) * lanes] = half[w * pairs : (w + 1) * pairs]
            return carry

        lax.fori_loop(0, tile // 2, six, 0, unroll=4)

        for r in range(0, blocks, 2):
            part = dot(lhs[...], left_ref[:, r * width : (r + 2) * width]).astype(jnp.bfloat16)
            made[r, at(piece), :] = part[:, :width]
            made[r + 1, at(piece), :] = part[:, width:]
        for r, sends in SCATTER_SENDS.items():

            @pl.when(me == r)
            def _(r=r, sends=sends):
                for slot, (row, owner) in enumerate(sends):
                    send(piece, r, slot, row, owner).start()

        @pl.when(piece >= 1)
        def _():
            hand(piece - 1)

        return carry

    lax.fori_loop(0, pieces, body, 0)
    hand(pieces - 1)

    def end(piece, carry):
        finish(piece)
        return carry

    lax.fori_loop(0, pieces, end, 0)
    for r, sends in SCATTER_SENDS.items():

        @pl.when(me == r)
        def _(r=r, sends=sends):
            def drain(piece, carry):
                for slot, (row, owner) in enumerate(sends):
                    send(piece, r, slot, row, owner).wait_send()
                if r in SCATTER_HANDS:
                    owner = SCATTER_HANDS[r]
                    send(piece, r, len(sends), owner, owner).wait_send()
                return carry

            lax.fori_loop(0, pieces, drain, 0)


def backward(right, residual, mpo, left, pairs, blocks, tile):
    parts, counts, _, lanes = residual.shape
    bonds, depth = right.shape[0] // PAD, right.shape[1]
    width = left.shape[1] // blocks
    pieces = bonds // tile
    steps = bonds * pairs
    flops = 2 * bonds * (PAD * depth * counts * lanes + mpo.size * lanes + pairs * left.size)
    size = 2 * (residual.size + left.size + right.size + steps * width)
    far = pl.BlockSpec(memory_space=pl.ANY)
    near = pl.BlockSpec(memory_space=pltpu.VMEM)
    return pl.pallas_call(
        functools.partial(backward_kernel, pieces),
        out_shape=jax.ShapeDtypeStruct((steps, width), jnp.bfloat16),
        in_specs=[far, far, near, far],
        out_specs=near,
        scratch_shapes=[
            pltpu.VMEM((2, tile * PAD, depth), jnp.bfloat16),
            pltpu.VMEM(residual.shape, jnp.bfloat16),
            pltpu.VMEM(left.shape, jnp.bfloat16),
            pltpu.VMEM((tile, counts, PAD, lanes), jnp.bfloat16),
            pltpu.VMEM((tile * pairs, left.shape[0]), jnp.bfloat16),
            pltpu.VMEM((blocks, steps, width), jnp.bfloat16),
            pltpu.VMEM((blocks, steps, width), jnp.bfloat16),
            pltpu.SemaphoreType.DMA((4, pieces)),
            pltpu.SemaphoreType.DMA((4, pieces)),
            pltpu.SemaphoreType.DMA((2,)),
            pltpu.SemaphoreType.DMA((2,)),
        ],
        compiler_params=pltpu.CompilerParams(
            collective_id=2, has_side_effects=True, vmem_limit_bytes=LIMIT
        ),
        cost_estimate=cost(flops, size),
    )(right, residual, mpo, left)


def mpo_product(mpo_left, mpo_right):
    paired = jnp.einsum("wuxs,uvyt->wstxyv", mpo_left, mpo_right, precision=lax.Precision.HIGHEST)
    channels, phys = mpo_left.shape[0], mpo_left.shape[2]
    return paired.reshape(channels * phys * phys, phys * phys * channels).astype(jnp.bfloat16)


def tiled_shards(theta, left_env, right_env, mpo_left, mpo_right):
    lanes, channels, depth = left_env.shape
    pairs, bonds = theta.shape[1:]
    width = theta.shape[0]
    blocks = lax.axis_size("row")
    cols, chans = lax.axis_size("col"), lax.axis_size("chan")
    parts = cols * chans
    tile = 32
    rows = right_env.shape[0]

    turned = jnp.transpose(theta, (2, 1, 0)).reshape(bonds * pairs, width)
    mpo = mpo_product(mpo_left, mpo_right).reshape(channels * pairs, pairs, channels)
    mpo = jnp.pad(mpo, ((0, 0), (0, 0), (0, PAD - channels)))
    mpo_back = mpo.reshape(channels * pairs, pairs * PAD)
    mpo_front = mpo_back.T
    left_back = jnp.transpose(left_env, (1, 0, 2)).reshape(channels * lanes, depth)
    right_back = jnp.transpose(right_env, (2, 1, 0))
    right_back = jnp.pad(right_back, ((0, 0), (0, PAD - channels), (0, 0)))
    right_back = right_back.reshape(bonds * PAD, rows)
    right_front = right_back.T

    total = forward(turned, left_back, mpo_front, right_front, pairs, tile, parts)
    full = exchange(total.reshape(cols, chans, pairs, rows // parts, lanes))
    mine = lax.axis_index("col") * chans + lax.axis_index("chan")
    kept = lax.dynamic_index_in_dim(full, mine, 0, keepdims=False)
    product = backward(right_back, full, mpo_back, left_back, pairs, blocks, tile)
    product = product.reshape(bonds, pairs, width)
    residual = jnp.transpose(kept, (1, 2, 0))
    return residual.reshape(rows // parts, lanes * pairs), jnp.transpose(product, (2, 1, 0))


def plain_shards(theta, left_env, right_env, mpo_left, mpo_right):
    left_rows, channels = left_env.shape[:2]
    pairs, right_rows = theta.shape[1:]
    mpo_pair = mpo_product(mpo_left, mpo_right)
    einsum = functools.partial(jnp.einsum, preferred_element_type=jnp.float32)
    one = einsum("awk,ksb->awsb", left_env, lax.all_gather(theta, "row", axis=0, tiled=True))
    one = one.astype(jnp.bfloat16).reshape(left_rows, channels * pairs, right_rows)
    three = einsum("pq,apb->aqb", mpo_pair, one).astype(jnp.bfloat16)
    three = three.reshape(left_rows, pairs, channels, right_rows)
    term = einsum("kvb,asvb->kas", right_env, three).astype(jnp.bfloat16)
    term = term.reshape(right_env.shape[0], left_rows * pairs)
    residual = lax.psum_scatter(term, ("col", "chan"), scatter_dimension=0, tiled=True)
    full = lax.all_gather(residual, ("col", "chan"), axis=0, tiled=True)
    back = einsum("kp,kvb->pvb", full, right_env).astype(jnp.bfloat16)
    back = back.reshape(left_rows, pairs * channels, right_rows)
    back = einsum("pq,aqb->apb", mpo_pair, back).astype(jnp.bfloat16)
    back = back.reshape(left_rows, channels, pairs, right_rows)
    product = einsum("awk,awsb->ksb", left_env, back).astype(jnp.bfloat16)
    return residual, lax.psum_scatter(product, "row", scatter_dimension=0, tiled=True)


def shards(theta, left_env, right_env, mpo_left, mpo_right):
    wide = left_env.shape[0] % 128 == 0 and theta.shape[0] % 128 == 0
    wide = wide and theta.shape[2] % 128 == 0 and theta.shape[1] == PAD
    wide = wide and lax.axis_size("col") == 2 and lax.axis_size("chan") == 2
    wide = wide and left_env.shape[1] % 2 == 0 and lax.axis_size("row") == 4
    wide = wide and left_env.shape[0] == theta.shape[0] and theta.shape[2] % 32 == 0
    body = tiled_shards if wide and left_env.shape[1] <= PAD else plain_shards
    return body(theta, left_env, right_env, mpo_left, mpo_right)


def solution(mesh):
    in_specs = (
        P(("grp", "row"), None, ("col", "chan")),
        P(("grp", "row"), None, None),
        P("grp", None, ("col", "chan")),
        P(),
        P(),
    )
    out_specs = (P(("grp", "col", "chan"), "row"), P(("grp", "row"), None, ("col", "chan")))
    return jax.shard_map(shards, mesh=mesh, in_specs=in_specs, out_specs=out_specs, check_vma=False)
```

```python
import functools

import jax
import jax.numpy as jnp
from jax import lax
from jax.experimental import pallas as pl
from jax.experimental.pallas import tpu as pltpu
from jax.sharding import PartitionSpec as P

LANES = 128
AHEAD = 3
LIMIT = 60 * 1024 * 1024
MESH = pl.DeviceIdType.MESH


def cost(flops, size):
    return pl.CostEstimate(flops=int(flops), bytes_accessed=int(size), transcendentals=0)


def dot(lhs, rhs):
    return jnp.dot(lhs, rhs, preferred_element_type=jnp.float32)


def greet(peers):
    barrier = pltpu.get_barrier_semaphore()
    for peer in peers:
        pl.semaphore_signal(barrier, inc=1, device_id=peer, device_id_type=MESH)
    pl.semaphore_wait(barrier, len(peers))


def row_peers():
    size = lax.axis_size("row")
    return [{"row": lax.rem(lax.axis_index("row") + step, size)} for step in range(1, size)]


def remote(source, target, send_sem, recv_sem, peer):
    return pltpu.make_async_remote_copy(
        src_ref=source,
        dst_ref=target,
        send_sem=send_sem,
        recv_sem=recv_sem,
        device_id=peer,
        device_id_type=MESH,
    )


GATHER_SENDS = {0: (1, 2), 1: (2, 0, 3), 2: (1, 3, 0), 3: (2, 1)}
GATHER_HANDS = {1: (3, 0), 2: (0, 3)}


def forward_kernel(
    pieces, theta_ref, left_hbm, mpo_ref, right_hbm, full_ref, turned_ref,
    gathered, left_ref, right_ref, held, wide, three, terms,
    sent, got, local, turns, swap_sent, swap_got, keeps, free,
):
    width = theta_ref.shape[1]
    tile, channels, pairs, lanes = held.shape
    _, bonds, _ = three.shape
    rows = full_ref.shape[2]
    count = pairs // 2
    chans = full_ref.shape[3] // (2 * lanes)
    step = tile * pairs
    group = channels * tile
    me, col, chan = lax.axis_index("row"), lax.axis_index("col"), lax.axis_index("chan")
    core, chip = {"col": 1 - col}, {"chan": 1 - chan}
    loads = [
        pltpu.make_async_copy(
            right_hbm.at[v], right_ref.at[:, v * bonds : (v + 1) * bonds], local.at[2 + v]
        )
        for v in range(channels)
    ]
    loads.append(pltpu.make_async_copy(left_hbm, left_ref, local.at[0]))
    for item in loads:
        item.start()

    def at(piece):
        return pl.ds(pl.multiple_of(piece * step, step), step)

    def block(piece, origin):
        return gathered.at[at(piece), origin * width : (origin + 1) * width]

    def send(piece, origin, slot, row, source=None):
        source = theta_ref.at[at(piece), :] if source is None else source
        return remote(
            source, block(piece, origin), sent.at[slot, piece], got.at[origin, piece], {"row": row}
        )

    def arrival(piece, origin):
        return send(piece, origin, 0, me)

    greet(row_peers() + [core, chip])
    for r, rows_to in GATHER_SENDS.items():

        @pl.when(me == r)
        def _(r=r, rows_to=rows_to):
            for piece in range(min(AHEAD, pieces)):
                for slot, row in enumerate(rows_to):
                    send(piece, r, slot, row).start()
            mine = pltpu.make_async_copy(
                theta_ref, gathered.at[:, r * width : (r + 1) * width], local.at[1]
            )
            mine.start()
            mine.wait()

    for item in loads:
        item.wait()

    def turned(v):
        where = pl.ds(pl.multiple_of(v * bonds, bonds), bonds)
        return pltpu.make_async_copy(terms.at[lax.rem(v, 2), 0], turned_ref.at[where, :], turns.at[lax.rem(v, 2)])

    def turn(v, carry):
        @pl.when(v >= 2)
        def _():
            turned(v - 2).wait()

        where = pl.ds(pl.multiple_of(v * bonds, bonds), bonds)
        terms[lax.rem(v, 2), 0] = right_ref[:, where].T
        turned(v).start()
        return carry

    lax.fori_loop(0, channels, turn, 0)
    for v in range(channels - 2, channels):
        turned(v).wait()

    def body(piece, carry):
        for r, rows_to in GATHER_SENDS.items():

            @pl.when(me == r)
            def _(r=r, rows_to=rows_to):
                late = [origin for origin in range(4) if origin != r]
                if r in GATHER_HANDS:
                    origin, row = GATHER_HANDS[r]
                    arrival(piece, origin).wait_recv()
                    send(piece, origin, len(rows_to), row, block(piece, origin)).start()
                    late.remove(origin)
                for origin in late:
                    arrival(piece, origin).wait_recv()

                @pl.when(piece + AHEAD < pieces)
                def _():
                    for slot, row in enumerate(rows_to):
                        send(piece + AHEAD, r, slot, row).start()

        def one(w, carry):
            where = pl.ds(pl.multiple_of(2 * w * lanes, 2 * lanes), 2 * lanes)
            part = lax.dot_general(
                gathered[at(piece), :],
                left_ref[where, :],
                (((1,), (1,)), ((), ())),
                preferred_element_type=jnp.float32,
            ).astype(jnp.bfloat16)
            held[:, 2 * w] = part[:, :lanes].reshape(tile, pairs, lanes)
            held[:, 2 * w + 1] = part[:, lanes:].reshape(tile, pairs, lanes)
            return carry

        lax.fori_loop(0, channels // 2, one, 0, unroll=2)

        def two(b, carry):
            first = held[2 * b].reshape(channels * pairs, lanes)
            second = held[2 * b + 1].reshape(channels * pairs, lanes)
            part = dot(mpo_ref[...], jnp.concatenate([first, second], axis=1))
            for j in range(2):
                where = pl.ds(2 * b + j, channels * pairs, stride=tile)
                for h in range(lanes // LANES):
                    begin = j * lanes + h * LANES
                    wide.at[h][where, :] = part[:, begin : begin + LANES]
            return carry

        lax.fori_loop(0, tile // 2, two, 0, unroll=4)

        def pack(x, carry):
            own = pl.ds(pl.multiple_of(x * group, group), group)
            where = pl.ds(pl.multiple_of(piece * tile, tile), tile)
            for h in range(lanes // LANES):
                part = wide[h, own, :].astype(jnp.bfloat16).reshape(channels, tile, LANES)
                three[pl.ds(x * channels, channels), where, h * LANES : (h + 1) * LANES] = part
            return carry

        lax.fori_loop(0, pairs, pack, 0)
        return carry

    lax.fori_loop(0, pieces, body, 0)
    for r, rows_to in GATHER_SENDS.items():

        @pl.when(me == r)
        def _(r=r, rows_to=rows_to):
            def finish(piece, carry):
                for slot, row in enumerate(rows_to):
                    send(piece, r, slot, row).wait_send()
                if r in GATHER_HANDS:
                    origin, row = GATHER_HANDS[r]
                    send(piece, origin, len(rows_to), row, block(piece, origin)).wait_send()
                return carry

            lax.fori_loop(0, pieces, finish, 0)

    pl.semaphore_signal(free.at[0], inc=1, device_id=core, device_id_type=MESH)
    pl.semaphore_signal(free.at[1], inc=1, device_id=chip, device_id_type=MESH)

    def near(p):
        return gathered.at[pl.ds(pl.multiple_of(p * rows, rows), rows), :]

    def far(p):
        return gathered.at[pl.ds(pl.multiple_of((count + p) * rows, rows), rows), :]

    def to_core(p):
        slot = lax.rem(p, 2)
        return remote(
            terms.at[slot, 1 - col], near(p), swap_sent.at[0, p], swap_got.at[0, p], core
        )

    def to_chip(p):
        return remote(near(p), far(p), swap_sent.at[1, p], swap_got.at[1, p], chip)

    def back(p):
        return remote(far(p), full_ref.at[p, col], swap_sent.at[2, p], swap_got.at[2, p], core)

    def keep(p):
        return pltpu.make_async_copy(far(p), full_ref.at[p, col], keeps.at[p])

    def term(p):
        depth = channels * bonds
        sides = [
            three[pl.ds((2 * p + j) * channels, channels)].reshape(depth, lanes) for j in range(2)
        ]
        value = dot(right_ref[...], jnp.concatenate(sides, axis=1)).astype(jnp.bfloat16)
        slot = lax.rem(p, 2)
        for c in range(2):
            for d in range(chans):
                part = value[(c * chans + d) * rows : (c * chans + d + 1) * rows]
                terms[slot, c, :, d * 2 * lanes : (d + 1) * 2 * lanes] = part

    def join(p):
        to_core(p).wait_recv()
        value = near(p)[...].astype(jnp.float32) + terms[lax.rem(p, 2), col].astype(jnp.float32)
        near(p)[...] = value.astype(jnp.bfloat16)

        @pl.when(p == 0)
        def _():
            pl.semaphore_wait(free.at[1], 1)

        to_chip(p).start()

    def close(p):
        to_chip(p).wait_recv()
        value = near(p)[...].astype(jnp.float32) + far(p)[...].astype(jnp.float32)
        far(p)[...] = value.astype(jnp.bfloat16)
        back(p).start()
        keep(p).start()

    def trade(p, carry):
        @pl.when(p < count)
        def _():
            @pl.when(p >= 2)
            def _():
                to_core(p - 2).wait_send()

            term(p)

            @pl.when(p == 0)
            def _():
                pl.semaphore_wait(free.at[0], 1)

            to_core(p).start()

        @pl.when((p >= 1) & (p <= count))
        def _():
            join(p - 1)

        @pl.when(p >= 3)
        def _():
            close(p - 3)

        return carry

    lax.fori_loop(0, count + 3, trade, 0)

    def finish(p, carry):
        @pl.when(p >= count - 2)
        def _():
            to_core(p).wait_send()

        to_chip(p).wait_send()
        back(p).wait_send()
        back(p).wait_recv()
        keep(p).wait()
        return carry

    lax.fori_loop(0, count, finish, 0)


def forward(theta, left, mpo, right, pairs, tile):
    steps, width = theta.shape
    channels, rows, bonds = right.shape
    depth, lanes = left.shape[1], width
    pieces = bonds // tile
    cols, chans = lax.axis_size("col"), lax.axis_size("chan")
    count, own = pairs // 2, rows // (cols * chans)
    flops = 2 * steps * left.size + 2 * bonds * mpo.size * lanes
    flops += 2 * right.size * pairs * lanes
    size = 2 * (theta.size + left.size + 2 * right.size) + 2 * rows * pairs * lanes
    far = pl.BlockSpec(memory_space=pl.ANY)
    return pl.pallas_call(
        functools.partial(forward_kernel, pieces),
        out_shape=[
            jax.ShapeDtypeStruct((count, cols, own, chans * 2 * lanes), jnp.bfloat16),
            jax.ShapeDtypeStruct((channels * bonds, rows), jnp.bfloat16),
        ],
        in_specs=[far, far, pl.BlockSpec(memory_space=pltpu.VMEM), far],
        out_specs=[far, far],
        scratch_shapes=[
            pltpu.VMEM((steps, depth), jnp.bfloat16),
            pltpu.VMEM(left.shape, jnp.bfloat16),
            pltpu.VMEM((rows, channels * bonds), jnp.bfloat16),
            pltpu.VMEM((tile, channels, pairs, lanes), jnp.bfloat16),
            pltpu.VMEM((lanes // LANES, channels * pairs * tile, LANES), jnp.float32),
            pltpu.VMEM((channels * pairs, bonds, lanes), jnp.bfloat16),
            pltpu.VMEM((2, cols, own, chans * 2 * lanes), jnp.bfloat16),
            pltpu.SemaphoreType.DMA((4, pieces)),
            pltpu.SemaphoreType.DMA((4, pieces)),
            pltpu.SemaphoreType.DMA((2 + channels,)),
            pltpu.SemaphoreType.DMA((2,)),
            pltpu.SemaphoreType.DMA((3, count)),
            pltpu.SemaphoreType.DMA((3, count)),
            pltpu.SemaphoreType.DMA((count,)),
            pltpu.SemaphoreType.REGULAR((2,)),
        ],
        compiler_params=pltpu.CompilerParams(
            collective_id=1, has_side_effects=True, vmem_limit_bytes=LIMIT
        ),
        cost_estimate=cost(flops, size),
    )(theta, left, mpo, right)


SCATTER_SENDS = {
    0: ((1, 3), (1, 1), (2, 2)),
    1: ((2, 2), (0, 0)),
    2: ((1, 1), (3, 3)),
    3: ((2, 0), (2, 2), (1, 1)),
}
SCATTER_HANDS = {1: 3, 2: 0}
SCATTER_FROM = {0: (1, 2), 1: (0, 2, 3), 2: (3, 1, 0), 3: (2, 1)}


def backward_kernel(
    pieces, right_hbm, res_hbm, mpo_ref, left_hbm, out_ref, kept_ref,
    right_ref, res_ref, left_ref, wide, lhs, made, come, sent, got, local, loads,
):
    _, channels, tile, depth = right_ref.shape
    lanes = wide.shape[0] * LANES
    pairs = lhs.shape[0] // tile
    count, cols, rows, _ = res_ref.shape
    chans = depth // (cols * rows)
    width = out_ref.shape[1]
    blocks = made.shape[0]
    step = tile * pairs
    group = channels * tile
    me = lax.axis_index("row")

    def load(piece, slot):
        where = pl.ds(pl.multiple_of(piece * tile, tile), tile)
        return pltpu.make_async_copy(right_hbm.at[:, where, :], right_ref.at[slot], loads.at[slot])

    load(0, 0).start()
    wholes = [
        pltpu.make_async_copy(res_hbm, res_ref, local.at[0]),
        pltpu.make_async_copy(left_hbm, left_ref, local.at[1]),
    ]
    for item in wholes:
        item.start()
    greet(row_peers())

    def at(piece):
        return pl.ds(pl.multiple_of(piece * step, step), step)

    def send(piece, r, slot, row, owner):
        place = r if row == owner else row
        target = come.at[place, at(piece), :]
        sems = sent.at[slot, piece], got.at[place, piece]
        return remote(made.at[owner, at(piece), :], target, *sems, {"row": row})

    def arrival(piece, place):
        target = come.at[place, at(piece), :]
        return remote(target, target, sent.at[0, piece], got.at[place, piece], {"row": me})

    def hand(piece):
        for r, owner in SCATTER_HANDS.items():

            @pl.when(me == r)
            def _(r=r, owner=owner):
                arrival(piece, r).wait_recv()
                value = made[owner, at(piece), :].astype(jnp.float32)
                value = value + come[r, at(piece), :].astype(jnp.float32)
                made[owner, at(piece), :] = value.astype(jnp.bfloat16)
                send(piece, r, len(SCATTER_SENDS[r]), owner, owner).start()

    def finish(piece):
        for r, origins in SCATTER_FROM.items():

            @pl.when(me == r)
            def _(r=r, origins=origins):
                for place in origins:
                    arrival(piece, place).wait_recv()
                value = made[r, at(piece), :].astype(jnp.float32)
                for place in origins:
                    value = value + come[place, at(piece), :].astype(jnp.float32)
                out_ref[at(piece), :] = value.astype(jnp.bfloat16)

    for item in wholes:
        item.wait()

    def body(piece, carry):
        now = lax.rem(piece, 2)
        load(piece, now).wait()

        @pl.when(piece + 1 < pieces)
        def _():
            load(piece + 1, 1 - now).start()

        def five(p, carry):
            half = 2 * lanes
            parts = [
                res_ref[p, c, :, d * half : (d + 1) * half] for c in range(cols) for d in range(chans)
            ]
            part = dot(right_ref[now].reshape(group, depth), jnp.concatenate(parts, axis=0))
            for j in range(2):
                where = pl.ds(pl.multiple_of((2 * p + j) * group, group), group)
                for h in range(lanes // LANES):
                    begin = j * lanes + h * LANES
                    wide[h, where, :] = part[:, begin : begin + LANES]
            return carry

        lax.fori_loop(0, count, five, 0, unroll=2)

        def six(b, carry):
            sides = []
            for j in range(2):
                where = pl.ds(2 * b + j, channels * pairs, stride=tile)
                for h in range(lanes // LANES):
                    sides.append(wide.at[h][where, :].astype(jnp.bfloat16))
            part = dot(mpo_ref[...], jnp.concatenate(sides, axis=1)).astype(jnp.bfloat16)
            for j in range(2):
                where = pl.ds(pl.multiple_of((2 * b + j) * pairs, pairs), pairs)
                half = part[:, j * lanes : (j + 1) * lanes]
                for w in range(channels):
                    lhs[where, w * lanes : (w + 1) * lanes] = half[w * pairs : (w + 1) * pairs]
            return carry

        lax.fori_loop(0, tile // 2, six, 0, unroll=4)

        for r in range(0, blocks, 2):
            part = dot(lhs[...], left_ref[:, r * width : (r + 2) * width]).astype(jnp.bfloat16)
            made[r, at(piece), :] = part[:, :width]
            made[r + 1, at(piece), :] = part[:, width:]
        for r, sends in SCATTER_SENDS.items():

            @pl.when(me == r)
            def _(r=r, sends=sends):
                for slot, (row, owner) in enumerate(sends):
                    send(piece, r, slot, row, owner).start()

        @pl.when(piece >= 1)
        def _():
            hand(piece - 1)

        return carry

    lax.fori_loop(0, pieces, body, 0)
    hand(pieces - 1)

    col, begin = lax.axis_index("col"), lax.axis_index("chan") * 2 * lanes
    for h in range(lanes // LANES):
        sides = [
            res_ref[x // 2, col, :, pl.ds(pl.multiple_of(begin + x % 2 * lanes + h * LANES, LANES), LANES)]
            for x in range(pairs)
        ]
        side = jnp.concatenate(sides, axis=1)

        def pick(t, carry, h=h, side=side):
            shape = (pairs * LANES, 2 * LANES)
            source = lax.broadcasted_iota(jnp.int32, shape, 0)
            target = lax.broadcasted_iota(jnp.int32, shape, 1) + t * 2 * LANES
            wanted = target % pairs * LANES + target // pairs
            chosen = jnp.where(source == wanted, 1.0, 0.0).astype(jnp.bfloat16)
            where = pl.multiple_of(h * LANES * pairs + t * 2 * LANES, 2 * LANES)
            kept_ref[:, pl.ds(where, 2 * LANES)] = dot(side, chosen).astype(jnp.bfloat16)
            return carry

        lax.fori_loop(0, pairs // 2, pick, 0)

    def end(piece, carry):
        finish(piece)
        return carry

    lax.fori_loop(0, pieces, end, 0)
    for r, sends in SCATTER_SENDS.items():

        @pl.when(me == r)
        def _(r=r, sends=sends):
            def drain(piece, carry):
                for slot, (row, owner) in enumerate(sends):
                    send(piece, r, slot, row, owner).wait_send()
                if r in SCATTER_HANDS:
                    owner = SCATTER_HANDS[r]
                    send(piece, r, len(sends), owner, owner).wait_send()
                return carry

            lax.fori_loop(0, pieces, drain, 0)


def backward(right, residual, mpo, left, pairs, blocks, tile):
    channels, bonds, depth = right.shape
    lanes = left.shape[0] // channels
    width = left.shape[1] // blocks
    pieces = bonds // tile
    steps = bonds * pairs
    flops = 2 * (right.size * pairs * lanes + bonds * mpo.size * lanes + steps * left.size)
    size = 2 * (residual.size + left.size + right.size + steps * width)
    far = pl.BlockSpec(memory_space=pl.ANY)
    near = pl.BlockSpec(memory_space=pltpu.VMEM)
    return pl.pallas_call(
        functools.partial(backward_kernel, pieces),
        out_shape=[
            jax.ShapeDtypeStruct((steps, width), jnp.bfloat16),
            jax.ShapeDtypeStruct((residual.shape[2], pairs * lanes), jnp.bfloat16),
        ],
        in_specs=[far, far, near, far],
        out_specs=[near, near],
        scratch_shapes=[
            pltpu.VMEM((2, channels, tile, depth), jnp.bfloat16),
            pltpu.VMEM(residual.shape, jnp.bfloat16),
            pltpu.VMEM(left.shape, jnp.bfloat16),
            pltpu.VMEM((lanes // LANES, channels * pairs * tile, LANES), jnp.float32),
            pltpu.VMEM((tile * pairs, left.shape[0]), jnp.bfloat16),
            pltpu.VMEM((blocks, steps, width), jnp.bfloat16),
            pltpu.VMEM((blocks, steps, width), jnp.bfloat16),
            pltpu.SemaphoreType.DMA((4, pieces)),
            pltpu.SemaphoreType.DMA((4, pieces)),
            pltpu.SemaphoreType.DMA((2,)),
            pltpu.SemaphoreType.DMA((2,)),
        ],
        compiler_params=pltpu.CompilerParams(
            collective_id=2, has_side_effects=True, vmem_limit_bytes=LIMIT
        ),
        cost_estimate=cost(flops, size),
    )(right, residual, mpo, left)


def mpo_product(mpo_left, mpo_right):
    paired = jnp.einsum("wuxs,uvyt->wstxyv", mpo_left, mpo_right, precision=lax.Precision.HIGHEST)
    channels, phys = mpo_left.shape[0], mpo_left.shape[2]
    return paired.reshape(channels * phys * phys, phys * phys * channels).astype(jnp.bfloat16)


def tiled_shards(theta, left_env, right_env, mpo_left, mpo_right):
    lanes, channels, depth = left_env.shape
    pairs, bonds = theta.shape[1:]
    width = theta.shape[0]
    blocks = lax.axis_size("row")
    tile = 32
    rows = right_env.shape[0]

    turned = jnp.transpose(theta, (2, 1, 0)).reshape(bonds * pairs, width)
    mpo = mpo_product(mpo_left, mpo_right)
    left = jnp.transpose(left_env, (1, 0, 2)).reshape(channels * lanes, depth)
    right = jnp.transpose(right_env, (1, 0, 2))

    full, right = forward(turned, left, mpo.T, right, pairs, tile)
    right = right.reshape(channels, bonds, rows)
    product, residual = backward(right, full, mpo, left, pairs, blocks, tile)
    return residual, jnp.transpose(product.reshape(bonds, pairs, width), (2, 1, 0))


def plain_shards(theta, left_env, right_env, mpo_left, mpo_right):
    left_rows, channels = left_env.shape[:2]
    pairs, right_rows = theta.shape[1:]
    mpo_pair = mpo_product(mpo_left, mpo_right)
    einsum = functools.partial(jnp.einsum, preferred_element_type=jnp.float32)
    one = einsum("awk,ksb->awsb", left_env, lax.all_gather(theta, "row", axis=0, tiled=True))
    one = one.astype(jnp.bfloat16).reshape(left_rows, channels * pairs, right_rows)
    three = einsum("pq,apb->aqb", mpo_pair, one).astype(jnp.bfloat16)
    three = three.reshape(left_rows, pairs, channels, right_rows)
    term = einsum("kvb,asvb->kas", right_env, three).astype(jnp.bfloat16)
    term = term.reshape(right_env.shape[0], left_rows * pairs)
    residual = lax.psum_scatter(term, ("col", "chan"), scatter_dimension=0, tiled=True)
    full = lax.all_gather(residual, ("col", "chan"), axis=0, tiled=True)
    back = einsum("kp,kvb->pvb", full, right_env).astype(jnp.bfloat16)
    back = back.reshape(left_rows, pairs * channels, right_rows)
    back = einsum("pq,aqb->apb", mpo_pair, back).astype(jnp.bfloat16)
    back = back.reshape(left_rows, channels, pairs, right_rows)
    product = einsum("awk,awsb->ksb", left_env, back).astype(jnp.bfloat16)
    return residual, lax.psum_scatter(product, "row", scatter_dimension=0, tiled=True)


def shards(theta, left_env, right_env, mpo_left, mpo_right):
    wide = left_env.shape[0] % 128 == 0 and theta.shape[0] % 128 == 0
    wide = wide and theta.shape[2] % 128 == 0 and theta.shape[1] == 16
    wide = wide and lax.axis_size("col") == 2 and lax.axis_size("chan") == 2
    wide = wide and left_env.shape[1] % 2 == 0 and lax.axis_size("row") == 4
    wide = wide and left_env.shape[0] == theta.shape[0] and theta.shape[2] % 32 == 0
    body = tiled_shards if wide and right_env.shape[0] == left_env.shape[2] else plain_shards
    return body(theta, left_env, right_env, mpo_left, mpo_right)


def solution(mesh):
    in_specs = (
        P(("grp", "row"), None, ("col", "chan")),
        P(("grp", "row"), None, None),
        P("grp", None, ("col", "chan")),
        P(),
        P(),
    )
    out_specs = (P(("grp", "col", "chan"), "row"), P(("grp", "row"), None, ("col", "chan")))
    return jax.shard_map(shards, mesh=mesh, in_specs=in_specs, out_specs=out_specs, check_vma=False)
```

```python
import functools

import jax
import jax.numpy as jnp
from jax import lax
from jax.experimental import pallas as pl
from jax.experimental.pallas import tpu as pltpu
from jax.sharding import PartitionSpec as P

LANES = 128
AHEAD = 3
LIMIT = 60 * 1024 * 1024
MESH = pl.DeviceIdType.MESH


def cost(flops, size):
    return pl.CostEstimate(flops=int(flops), bytes_accessed=int(size), transcendentals=0)


def dot(lhs, rhs):
    return jnp.dot(lhs, rhs, preferred_element_type=jnp.float32)


def greet(peers):
    barrier = pltpu.get_barrier_semaphore()
    for peer in peers:
        pl.semaphore_signal(barrier, inc=1, device_id=peer, device_id_type=MESH)
    pl.semaphore_wait(barrier, len(peers))


def row_peers():
    size = lax.axis_size("row")
    return [{"row": lax.rem(lax.axis_index("row") + step, size)} for step in range(1, size)]


def remote(source, target, send_sem, recv_sem, peer):
    return pltpu.make_async_remote_copy(
        src_ref=source,
        dst_ref=target,
        send_sem=send_sem,
        recv_sem=recv_sem,
        device_id=peer,
        device_id_type=MESH,
    )


GATHER_SENDS = {0: (1, 2), 1: (2, 0, 3), 2: (1, 3, 0), 3: (2, 1)}
GATHER_HANDS = {1: (3, 0), 2: (0, 3)}


def forward_kernel(
    pieces, theta_ref, left_hbm, mpo_ref, right_hbm, full_ref, turned_ref,
    gathered, left_ref, right_ref, held, wide, three, terms,
    sent, got, local, turns, swap_sent, swap_got, keeps, free,
):
    width = theta_ref.shape[1]
    tile, channels, pairs, lanes = held.shape
    _, bonds, _ = three.shape
    rows = full_ref.shape[2]
    count = pairs // 2
    chans = full_ref.shape[3] // (2 * lanes)
    step = tile * pairs
    group = channels * tile
    me, col, chan = lax.axis_index("row"), lax.axis_index("col"), lax.axis_index("chan")
    core, chip = {"col": 1 - col}, {"chan": 1 - chan}
    loads = [
        pltpu.make_async_copy(
            right_hbm.at[v], right_ref.at[:, v * bonds : (v + 1) * bonds], local.at[2 + v]
        )
        for v in range(channels)
    ]
    loads.append(pltpu.make_async_copy(left_hbm, left_ref, local.at[0]))
    for item in loads:
        item.start()

    def at(piece):
        return pl.ds(pl.multiple_of(piece * step, step), step)

    def block(piece, origin):
        return gathered.at[at(piece), origin * width : (origin + 1) * width]

    def send(piece, origin, slot, row, source=None):
        source = theta_ref.at[at(piece), :] if source is None else source
        return remote(
            source, block(piece, origin), sent.at[slot, piece], got.at[origin, piece], {"row": row}
        )

    def arrival(piece, origin):
        return send(piece, origin, 0, me)

    greet(row_peers() + [core, chip])
    for r, rows_to in GATHER_SENDS.items():

        @pl.when(me == r)
        def _(r=r, rows_to=rows_to):
            for piece in range(min(AHEAD, pieces)):
                for slot, row in enumerate(rows_to):
                    send(piece, r, slot, row).start()
            mine = pltpu.make_async_copy(
                theta_ref, gathered.at[:, r * width : (r + 1) * width], local.at[1]
            )
            mine.start()
            mine.wait()

    for item in loads:
        item.wait()

    def turned(v):
        where = pl.ds(pl.multiple_of(v * bonds, bonds), bonds)
        return pltpu.make_async_copy(terms.at[lax.rem(v, 2), 0], turned_ref.at[where, :], turns.at[lax.rem(v, 2)])

    def turn(v, carry):
        @pl.when(v >= 2)
        def _():
            turned(v - 2).wait()

        where = pl.ds(pl.multiple_of(v * bonds, bonds), bonds)
        terms[lax.rem(v, 2), 0] = right_ref[:, where].T
        turned(v).start()
        return carry

    lax.fori_loop(0, channels, turn, 0)
    for v in range(channels - 2, channels):
        turned(v).wait()

    def body(piece, carry):
        for r, rows_to in GATHER_SENDS.items():

            @pl.when(me == r)
            def _(r=r, rows_to=rows_to):
                late = [origin for origin in range(4) if origin != r]
                if r in GATHER_HANDS:
                    origin, row = GATHER_HANDS[r]
                    arrival(piece, origin).wait_recv()
                    send(piece, origin, len(rows_to), row, block(piece, origin)).start()
                    late.remove(origin)
                for origin in late:
                    arrival(piece, origin).wait_recv()

                @pl.when(piece + AHEAD < pieces)
                def _():
                    for slot, row in enumerate(rows_to):
                        send(piece + AHEAD, r, slot, row).start()

        def one(w, carry):
            where = pl.ds(pl.multiple_of(2 * w * lanes, 2 * lanes), 2 * lanes)
            part = lax.dot_general(
                gathered[at(piece), :],
                left_ref[where, :],
                (((1,), (1,)), ((), ())),
                preferred_element_type=jnp.float32,
            ).astype(jnp.bfloat16)
            held[:, 2 * w] = part[:, :lanes].reshape(tile, pairs, lanes)
            held[:, 2 * w + 1] = part[:, lanes:].reshape(tile, pairs, lanes)
            return carry

        lax.fori_loop(0, channels // 2, one, 0, unroll=2)

        def two(b, carry):
            first = held[2 * b].reshape(channels * pairs, lanes)
            second = held[2 * b + 1].reshape(channels * pairs, lanes)
            part = dot(mpo_ref[...], jnp.concatenate([first, second], axis=1))
            for j in range(2):
                where = pl.ds(2 * b + j, channels * pairs, stride=tile)
                for h in range(lanes // LANES):
                    begin = j * lanes + h * LANES
                    wide.at[h][where, :] = part[:, begin : begin + LANES]
            return carry

        lax.fori_loop(0, tile // 2, two, 0, unroll=4)

        def pack(x, carry):
            own = pl.ds(pl.multiple_of(x * group, group), group)
            where = pl.ds(pl.multiple_of(piece * tile, tile), tile)
            for h in range(lanes // LANES):
                part = wide[h, own, :].astype(jnp.bfloat16).reshape(channels, tile, LANES)
                three[pl.ds(x * channels, channels), where, h * LANES : (h + 1) * LANES] = part
            return carry

        lax.fori_loop(0, pairs, pack, 0)
        return carry

    lax.fori_loop(0, pieces, body, 0)
    for r, rows_to in GATHER_SENDS.items():

        @pl.when(me == r)
        def _(r=r, rows_to=rows_to):
            def finish(piece, carry):
                for slot, row in enumerate(rows_to):
                    send(piece, r, slot, row).wait_send()
                if r in GATHER_HANDS:
                    origin, row = GATHER_HANDS[r]
                    send(piece, origin, len(rows_to), row, block(piece, origin)).wait_send()
                return carry

            lax.fori_loop(0, pieces, finish, 0)

    pl.semaphore_signal(free.at[0], inc=1, device_id=core, device_id_type=MESH)
    pl.semaphore_signal(free.at[1], inc=1, device_id=chip, device_id_type=MESH)

    def near(p):
        return gathered.at[pl.ds(pl.multiple_of(p * rows, rows), rows), :]

    def far(p):
        return gathered.at[pl.ds(pl.multiple_of((count + p) * rows, rows), rows), :]

    def to_core(p):
        slot = lax.rem(p, 2)
        return remote(
            terms.at[slot, 1 - col], near(p), swap_sent.at[0, p], swap_got.at[0, p], core
        )

    def to_chip(p):
        return remote(near(p), far(p), swap_sent.at[1, p], swap_got.at[1, p], chip)

    def back(p):
        return remote(far(p), full_ref.at[p, col], swap_sent.at[2, p], swap_got.at[2, p], core)

    def keep(p):
        return pltpu.make_async_copy(far(p), full_ref.at[p, col], keeps.at[p])

    def term(p):
        depth = channels * bonds
        sides = [
            three[pl.ds((2 * p + j) * channels, channels)].reshape(depth, lanes) for j in range(2)
        ]
        value = dot(right_ref[...], jnp.concatenate(sides, axis=1)).astype(jnp.bfloat16)
        slot = lax.rem(p, 2)
        for c in range(2):
            for d in range(chans):
                part = value[(c * chans + d) * rows : (c * chans + d + 1) * rows]
                terms[slot, c, :, d * 2 * lanes : (d + 1) * 2 * lanes] = part

    def join(p):
        to_core(p).wait_recv()
        value = near(p)[...].astype(jnp.float32) + terms[lax.rem(p, 2), col].astype(jnp.float32)
        near(p)[...] = value.astype(jnp.bfloat16)

        @pl.when(p == 0)
        def _():
            pl.semaphore_wait(free.at[1], 1)

        to_chip(p).start()

    def close(p):
        to_chip(p).wait_recv()
        value = near(p)[...].astype(jnp.float32) + far(p)[...].astype(jnp.float32)
        far(p)[...] = value.astype(jnp.bfloat16)
        back(p).start()
        keep(p).start()

    def trade(p, carry):
        @pl.when(p < count)
        def _():
            @pl.when(p >= 2)
            def _():
                to_core(p - 2).wait_send()

            term(p)

            @pl.when(p == 0)
            def _():
                pl.semaphore_wait(free.at[0], 1)

            to_core(p).start()

        @pl.when((p >= 1) & (p <= count))
        def _():
            join(p - 1)

        @pl.when(p >= 3)
        def _():
            close(p - 3)

        return carry

    lax.fori_loop(0, count + 3, trade, 0)

    def finish(p, carry):
        @pl.when(p >= count - 2)
        def _():
            to_core(p).wait_send()

        to_chip(p).wait_send()
        back(p).wait_send()
        back(p).wait_recv()
        keep(p).wait()
        return carry

    lax.fori_loop(0, count, finish, 0)


def forward(theta, left, mpo, right, pairs, tile):
    steps, width = theta.shape
    channels, rows, bonds = right.shape
    depth, lanes = left.shape[1], width
    pieces = bonds // tile
    cols, chans = lax.axis_size("col"), lax.axis_size("chan")
    count, own = pairs // 2, rows // (cols * chans)
    flops = 2 * steps * left.size + 2 * bonds * mpo.size * lanes
    flops += 2 * right.size * pairs * lanes
    size = 2 * (theta.size + left.size + 2 * right.size) + 2 * rows * pairs * lanes
    far = pl.BlockSpec(memory_space=pl.ANY)
    return pl.pallas_call(
        functools.partial(forward_kernel, pieces),
        out_shape=[
            jax.ShapeDtypeStruct((count, cols, own, chans * 2 * lanes), jnp.bfloat16),
            jax.ShapeDtypeStruct((channels * bonds, rows), jnp.bfloat16),
        ],
        in_specs=[far, far, pl.BlockSpec(memory_space=pltpu.VMEM), far],
        out_specs=[far, far],
        scratch_shapes=[
            pltpu.VMEM((steps, depth), jnp.bfloat16),
            pltpu.VMEM(left.shape, jnp.bfloat16),
            pltpu.VMEM((rows, channels * bonds), jnp.bfloat16),
            pltpu.VMEM((tile, channels, pairs, lanes), jnp.bfloat16),
            pltpu.VMEM((lanes // LANES, channels * pairs * tile, LANES), jnp.float32),
            pltpu.VMEM((channels * pairs, bonds, lanes), jnp.bfloat16),
            pltpu.VMEM((2, cols, own, chans * 2 * lanes), jnp.bfloat16),
            pltpu.SemaphoreType.DMA((4, pieces)),
            pltpu.SemaphoreType.DMA((4, pieces)),
            pltpu.SemaphoreType.DMA((2 + channels,)),
            pltpu.SemaphoreType.DMA((2,)),
            pltpu.SemaphoreType.DMA((3, count)),
            pltpu.SemaphoreType.DMA((3, count)),
            pltpu.SemaphoreType.DMA((count,)),
            pltpu.SemaphoreType.REGULAR((2,)),
        ],
        compiler_params=pltpu.CompilerParams(
            collective_id=1, has_side_effects=True, vmem_limit_bytes=LIMIT
        ),
        cost_estimate=cost(flops, size),
    )(theta, left, mpo, right)


SCATTER_SENDS = {
    0: ((1, 3), (1, 1), (2, 2)),
    1: ((2, 2), (0, 0)),
    2: ((1, 1), (3, 3)),
    3: ((2, 0), (2, 2), (1, 1)),
}
SCATTER_HANDS = {1: 3, 2: 0}
SCATTER_FROM = {0: (1, 2), 1: (0, 2, 3), 2: (3, 1, 0), 3: (2, 1)}


def backward_kernel(
    pieces, right_hbm, res_hbm, mpo_ref, left_hbm, out_ref, kept_ref,
    right_ref, res_ref, left_ref, wide, lhs, made, come, sent, got, local, loads,
):
    _, channels, tile, depth = right_ref.shape
    lanes = wide.shape[0] * LANES
    pairs = lhs.shape[0] // tile
    count, cols, rows, _ = res_ref.shape
    chans = depth // (cols * rows)
    width = out_ref.shape[1]
    blocks = made.shape[0]
    step = tile * pairs
    group = channels * tile
    me = lax.axis_index("row")

    def load(piece, slot):
        where = pl.ds(pl.multiple_of(piece * tile, tile), tile)
        return pltpu.make_async_copy(right_hbm.at[:, where, :], right_ref.at[slot], loads.at[slot])

    load(0, 0).start()
    wholes = [
        pltpu.make_async_copy(res_hbm, res_ref, local.at[0]),
        pltpu.make_async_copy(left_hbm, left_ref, local.at[1]),
    ]
    for item in wholes:
        item.start()
    greet(row_peers())

    def at(piece):
        return pl.ds(pl.multiple_of(piece * step, step), step)

    def send(piece, r, slot, row, owner):
        place = r if row == owner else row
        target = come.at[place, at(piece), :]
        sems = sent.at[slot, piece], got.at[place, piece]
        return remote(made.at[owner, at(piece), :], target, *sems, {"row": row})

    def arrival(piece, place):
        target = come.at[place, at(piece), :]
        return remote(target, target, sent.at[0, piece], got.at[place, piece], {"row": me})

    def hand(piece):
        for r, owner in SCATTER_HANDS.items():

            @pl.when(me == r)
            def _(r=r, owner=owner):
                arrival(piece, r).wait_recv()
                value = made[owner, at(piece), :].astype(jnp.float32)
                value = value + come[r, at(piece), :].astype(jnp.float32)
                made[owner, at(piece), :] = value.astype(jnp.bfloat16)
                send(piece, r, len(SCATTER_SENDS[r]), owner, owner).start()

    def finish(piece):
        for r, origins in SCATTER_FROM.items():

            @pl.when(me == r)
            def _(r=r, origins=origins):
                for place in origins:
                    arrival(piece, place).wait_recv()
                value = made[r, at(piece), :].astype(jnp.float32)
                for place in origins:
                    value = value + come[place, at(piece), :].astype(jnp.float32)
                out_ref[at(piece), :] = value.astype(jnp.bfloat16)

    for item in wholes:
        item.wait()

    def body(piece, carry):
        now = lax.rem(piece, 2)
        load(piece, now).wait()

        @pl.when(piece + 1 < pieces)
        def _():
            load(piece + 1, 1 - now).start()

        def five(p, carry):
            half = 2 * lanes
            parts = [
                res_ref[p, c, :, d * half : (d + 1) * half] for c in range(cols) for d in range(chans)
            ]
            part = dot(right_ref[now].reshape(group, depth), jnp.concatenate(parts, axis=0))
            for j in range(2):
                where = pl.ds(pl.multiple_of((2 * p + j) * group, group), group)
                for h in range(lanes // LANES):
                    begin = j * lanes + h * LANES
                    wide[h, where, :] = part[:, begin : begin + LANES]
            return carry

        lax.fori_loop(0, count, five, 0, unroll=2)

        def six(b, carry):
            sides = []
            for j in range(2):
                where = pl.ds(2 * b + j, channels * pairs, stride=tile)
                for h in range(lanes // LANES):
                    sides.append(wide.at[h][where, :].astype(jnp.bfloat16))
            part = dot(mpo_ref[...], jnp.concatenate(sides, axis=1)).astype(jnp.bfloat16)
            for j in range(2):
                where = pl.ds(pl.multiple_of((2 * b + j) * pairs, pairs), pairs)
                half = part[:, j * lanes : (j + 1) * lanes]
                for w in range(channels):
                    lhs[where, w * lanes : (w + 1) * lanes] = half[w * pairs : (w + 1) * pairs]
            return carry

        lax.fori_loop(0, tile // 2, six, 0, unroll=4)

        for r in range(0, blocks, 2):
            part = dot(lhs[...], left_ref[:, r * width : (r + 2) * width]).astype(jnp.bfloat16)
            made[r, at(piece), :] = part[:, :width]
            made[r + 1, at(piece), :] = part[:, width:]
        for r, sends in SCATTER_SENDS.items():

            @pl.when(me == r)
            def _(r=r, sends=sends):
                for slot, (row, owner) in enumerate(sends):
                    send(piece, r, slot, row, owner).start()

        @pl.when(piece >= 1)
        def _():
            hand(piece - 1)

        return carry

    lax.fori_loop(0, pieces, body, 0)
    hand(pieces - 1)

    col, begin = lax.axis_index("col"), lax.axis_index("chan") * 2 * lanes
    for h in range(lanes // LANES):
        sides = [
            res_ref[x // 2, col, :, pl.ds(pl.multiple_of(begin + x % 2 * lanes + h * LANES, LANES), LANES)]
            for x in range(pairs)
        ]
        side = jnp.concatenate(sides, axis=1)

        def pick(t, carry, h=h, side=side):
            shape = (pairs * LANES, 2 * LANES)
            source = lax.broadcasted_iota(jnp.int32, shape, 0)
            target = lax.broadcasted_iota(jnp.int32, shape, 1) + t * 2 * LANES
            wanted = target % pairs * LANES + target // pairs
            chosen = jnp.where(source == wanted, 1.0, 0.0).astype(jnp.bfloat16)
            where = pl.multiple_of(h * LANES * pairs + t * 2 * LANES, 2 * LANES)
            kept_ref[:, pl.ds(where, 2 * LANES)] = dot(side, chosen).astype(jnp.bfloat16)
            return carry

        lax.fori_loop(0, pairs // 2, pick, 0)

    def end(piece, carry):
        finish(piece)
        return carry

    lax.fori_loop(0, pieces, end, 0)
    for r, sends in SCATTER_SENDS.items():

        @pl.when(me == r)
        def _(r=r, sends=sends):
            def drain(piece, carry):
                for slot, (row, owner) in enumerate(sends):
                    send(piece, r, slot, row, owner).wait_send()
                if r in SCATTER_HANDS:
                    owner = SCATTER_HANDS[r]
                    send(piece, r, len(sends), owner, owner).wait_send()
                return carry

            lax.fori_loop(0, pieces, drain, 0)


def backward(right, residual, mpo, left, pairs, blocks, tile):
    channels, bonds, depth = right.shape
    lanes = left.shape[0] // channels
    width = left.shape[1] // blocks
    pieces = bonds // tile
    steps = bonds * pairs
    flops = 2 * (right.size * pairs * lanes + bonds * mpo.size * lanes + steps * left.size)
    size = 2 * (residual.size + left.size + right.size + steps * width)
    far = pl.BlockSpec(memory_space=pl.ANY)
    near = pl.BlockSpec(memory_space=pltpu.VMEM)
    return pl.pallas_call(
        functools.partial(backward_kernel, pieces),
        out_shape=[
            jax.ShapeDtypeStruct((steps, width), jnp.bfloat16),
            jax.ShapeDtypeStruct((residual.shape[2], pairs * lanes), jnp.bfloat16),
        ],
        in_specs=[far, far, near, far],
        out_specs=[near, near],
        scratch_shapes=[
            pltpu.VMEM((2, channels, tile, depth), jnp.bfloat16),
            pltpu.VMEM(residual.shape, jnp.bfloat16),
            pltpu.VMEM(left.shape, jnp.bfloat16),
            pltpu.VMEM((lanes // LANES, channels * pairs * tile, LANES), jnp.float32),
            pltpu.VMEM((tile * pairs, left.shape[0]), jnp.bfloat16),
            pltpu.VMEM((blocks, steps, width), jnp.bfloat16),
            pltpu.VMEM((blocks, steps, width), jnp.bfloat16),
            pltpu.SemaphoreType.DMA((4, pieces)),
            pltpu.SemaphoreType.DMA((4, pieces)),
            pltpu.SemaphoreType.DMA((2,)),
            pltpu.SemaphoreType.DMA((2,)),
        ],
        compiler_params=pltpu.CompilerParams(
            collective_id=2, has_side_effects=True, vmem_limit_bytes=LIMIT
        ),
        cost_estimate=cost(flops, size),
    )(right, residual, mpo, left)


def mpo_product(mpo_left, mpo_right):
    paired = jnp.einsum("wuxs,uvyt->wstxyv", mpo_left, mpo_right, precision=lax.Precision.HIGHEST)
    channels, phys = mpo_left.shape[0], mpo_left.shape[2]
    return paired.reshape(channels * phys * phys, phys * phys * channels).astype(jnp.bfloat16)


def tiled_shards(theta, left_env, right_env, mpo_left, mpo_right):
    lanes, channels, depth = left_env.shape
    pairs, bonds = theta.shape[1:]
    width = theta.shape[0]
    blocks = lax.axis_size("row")
    tile = 16
    rows = right_env.shape[0]

    turned = jnp.transpose(theta, (2, 1, 0)).reshape(bonds * pairs, width)
    mpo = mpo_product(mpo_left, mpo_right)
    left = jnp.transpose(left_env, (1, 0, 2)).reshape(channels * lanes, depth)
    right = jnp.transpose(right_env, (1, 0, 2))

    full, right = forward(turned, left, mpo.T, right, pairs, tile)
    right = right.reshape(channels, bonds, rows)
    product, residual = backward(right, full, mpo, left, pairs, blocks, tile)
    return residual, jnp.transpose(product.reshape(bonds, pairs, width), (2, 1, 0))


def plain_shards(theta, left_env, right_env, mpo_left, mpo_right):
    left_rows, channels = left_env.shape[:2]
    pairs, right_rows = theta.shape[1:]
    mpo_pair = mpo_product(mpo_left, mpo_right)
    einsum = functools.partial(jnp.einsum, preferred_element_type=jnp.float32)
    one = einsum("awk,ksb->awsb", left_env, lax.all_gather(theta, "row", axis=0, tiled=True))
    one = one.astype(jnp.bfloat16).reshape(left_rows, channels * pairs, right_rows)
    three = einsum("pq,apb->aqb", mpo_pair, one).astype(jnp.bfloat16)
    three = three.reshape(left_rows, pairs, channels, right_rows)
    term = einsum("kvb,asvb->kas", right_env, three).astype(jnp.bfloat16)
    term = term.reshape(right_env.shape[0], left_rows * pairs)
    residual = lax.psum_scatter(term, ("col", "chan"), scatter_dimension=0, tiled=True)
    full = lax.all_gather(residual, ("col", "chan"), axis=0, tiled=True)
    back = einsum("kp,kvb->pvb", full, right_env).astype(jnp.bfloat16)
    back = back.reshape(left_rows, pairs * channels, right_rows)
    back = einsum("pq,aqb->apb", mpo_pair, back).astype(jnp.bfloat16)
    back = back.reshape(left_rows, channels, pairs, right_rows)
    product = einsum("awk,awsb->ksb", left_env, back).astype(jnp.bfloat16)
    return residual, lax.psum_scatter(product, "row", scatter_dimension=0, tiled=True)


def shards(theta, left_env, right_env, mpo_left, mpo_right):
    wide = left_env.shape[0] % 128 == 0 and theta.shape[0] % 128 == 0
    wide = wide and theta.shape[2] % 128 == 0 and theta.shape[1] == 16
    wide = wide and lax.axis_size("col") == 2 and lax.axis_size("chan") == 2
    wide = wide and left_env.shape[1] % 2 == 0 and lax.axis_size("row") == 4
    wide = wide and left_env.shape[0] == theta.shape[0] and theta.shape[2] % 32 == 0
    body = tiled_shards if wide and right_env.shape[0] == left_env.shape[2] else plain_shards
    return body(theta, left_env, right_env, mpo_left, mpo_right)


def solution(mesh):
    in_specs = (
        P(("grp", "row"), None, ("col", "chan")),
        P(("grp", "row"), None, None),
        P("grp", None, ("col", "chan")),
        P(),
        P(),
    )
    out_specs = (P(("grp", "col", "chan"), "row"), P(("grp", "row"), None, ("col", "chan")))
    return jax.shard_map(shards, mesh=mesh, in_specs=in_specs, out_specs=out_specs, check_vma=False)
```

```python
import functools

import jax
import jax.numpy as jnp
from jax import lax
from jax.experimental import pallas as pl
from jax.experimental.pallas import tpu as pltpu
from jax.sharding import PartitionSpec as P

LANES = 128
AHEAD = 3
LIMIT = 60 * 1024 * 1024
MESH = pl.DeviceIdType.MESH


def cost(flops, size):
    return pl.CostEstimate(flops=int(flops), bytes_accessed=int(size), transcendentals=0)


def dot(lhs, rhs):
    return jnp.dot(lhs, rhs, preferred_element_type=jnp.float32)


def greet(peers):
    barrier = pltpu.get_barrier_semaphore()
    for peer in peers:
        pl.semaphore_signal(barrier, inc=1, device_id=peer, device_id_type=MESH)
    pl.semaphore_wait(barrier, len(peers))


def row_peers():
    size = lax.axis_size("row")
    return [{"row": lax.rem(lax.axis_index("row") + step, size)} for step in range(1, size)]


def remote(source, target, send_sem, recv_sem, peer):
    return pltpu.make_async_remote_copy(
        src_ref=source,
        dst_ref=target,
        send_sem=send_sem,
        recv_sem=recv_sem,
        device_id=peer,
        device_id_type=MESH,
    )


GATHER_SENDS = {0: (1, 2), 1: (2, 0, 3), 2: (1, 3, 0), 3: (2, 1)}
GATHER_HANDS = {1: (3, 0), 2: (0, 3)}


SCATTER_SENDS = {
    0: ((1, 3), (1, 1), (2, 2)),
    1: ((2, 2), (0, 0)),
    2: ((1, 1), (3, 3)),
    3: ((2, 0), (2, 2), (1, 1)),
}
SCATTER_HANDS = {1: 3, 2: 0}
SCATTER_FROM = {0: (1, 2), 1: (0, 2, 3), 2: (3, 1, 0), 3: (2, 1)}


def kernel(
    pieces, theta_ref, left_hbm, front_ref, mpo_ref, right_hbm, out_ref, kept_ref, turned_hbm,
    gathered, left_ref, right_ref, held, wide, three, terms, turned_ref, lhs,
    sent, got, local, turns, swap_sent, swap_got, full_sent, full_got, keeps, free,
    gave, took, clear, reads,
):
    width = theta_ref.shape[1]
    tile, channels, pairs, lanes = held.shape
    _, bonds, _ = three.shape
    _, cols, rows, depth = terms.shape
    count = pairs // 2
    chans = depth // (2 * lanes)
    blocks = gathered.shape[1] // width
    step = tile * pairs
    group = channels * tile
    me, col, chan = lax.axis_index("row"), lax.axis_index("col"), lax.axis_index("chan")
    core, chip = {"col": 1 - col}, {"chan": 1 - chan}
    loads = [
        pltpu.make_async_copy(
            right_hbm.at[v], right_ref.at[:, v * bonds : (v + 1) * bonds], local.at[2 + v]
        )
        for v in range(channels)
    ]
    loads.append(pltpu.make_async_copy(left_hbm, left_ref, local.at[0]))
    for item in loads:
        item.start()

    def at(piece):
        return pl.ds(pl.multiple_of(piece * step, step), step)

    def block(piece, origin):
        return gathered.at[at(piece), origin * width : (origin + 1) * width]

    def send(piece, origin, slot, row, source=None):
        source = theta_ref.at[at(piece), :] if source is None else source
        return remote(
            source, block(piece, origin), sent.at[slot, piece], got.at[origin, piece], {"row": row}
        )

    def arrival(piece, origin):
        return send(piece, origin, 0, me)

    greet(row_peers() + [core, chip])
    for r, rows_to in GATHER_SENDS.items():

        @pl.when(me == r)
        def _(r=r, rows_to=rows_to):
            for piece in range(min(AHEAD, pieces)):
                for slot, row in enumerate(rows_to):
                    send(piece, r, slot, row).start()
            mine = pltpu.make_async_copy(
                theta_ref, gathered.at[:, r * width : (r + 1) * width], local.at[1]
            )
            mine.start()
            mine.wait()

    for item in loads:
        item.wait()

    def turned(v):
        slot = lax.rem(v, 2)
        return pltpu.make_async_copy(terms.at[slot, 0], turned_hbm.at[v], turns.at[slot])

    def turn(v, carry):
        @pl.when(v >= 2)
        def _():
            turned(v - 2).wait()

        where = pl.ds(pl.multiple_of(v * bonds, bonds), bonds)
        terms[lax.rem(v, 2), 0] = right_ref[:, where].T
        turned(v).start()
        return carry

    lax.fori_loop(0, channels, turn, 0)
    for v in range(channels - 2, channels):
        turned(v).wait()

    def body(piece, carry):
        for r, rows_to in GATHER_SENDS.items():

            @pl.when(me == r)
            def _(r=r, rows_to=rows_to):
                late = [origin for origin in range(4) if origin != r]
                if r in GATHER_HANDS:
                    origin, row = GATHER_HANDS[r]
                    arrival(piece, origin).wait_recv()
                    send(piece, origin, len(rows_to), row, block(piece, origin)).start()
                    late.remove(origin)
                for origin in late:
                    arrival(piece, origin).wait_recv()

                @pl.when(piece + AHEAD < pieces)
                def _():
                    for slot, row in enumerate(rows_to):
                        send(piece + AHEAD, r, slot, row).start()

        def one(w, carry):
            where = pl.ds(pl.multiple_of(2 * w * lanes, 2 * lanes), 2 * lanes)
            part = lax.dot_general(
                gathered[at(piece), :],
                left_ref[where, :],
                (((1,), (1,)), ((), ())),
                preferred_element_type=jnp.float32,
            ).astype(jnp.bfloat16)
            held[:, 2 * w] = part[:, :lanes].reshape(tile, pairs, lanes)
            held[:, 2 * w + 1] = part[:, lanes:].reshape(tile, pairs, lanes)
            return carry

        lax.fori_loop(0, channels // 2, one, 0, unroll=2)

        def two(b, carry):
            first = held[2 * b].reshape(channels * pairs, lanes)
            second = held[2 * b + 1].reshape(channels * pairs, lanes)
            part = dot(front_ref[...], jnp.concatenate([first, second], axis=1))
            for j in range(2):
                where = pl.ds(2 * b + j, channels * pairs, stride=tile)
                for h in range(lanes // LANES):
                    begin = j * lanes + h * LANES
                    wide.at[h][where, :] = part[:, begin : begin + LANES]
            return carry

        lax.fori_loop(0, tile // 2, two, 0, unroll=4)

        def pack(x, carry):
            own = pl.ds(pl.multiple_of(x * group, group), group)
            where = pl.ds(pl.multiple_of(piece * tile, tile), tile)
            for h in range(lanes // LANES):
                part = wide[h, own, :].astype(jnp.bfloat16).reshape(channels, tile, LANES)
                three[pl.ds(x * channels, channels), where, h * LANES : (h + 1) * LANES] = part
            return carry

        lax.fori_loop(0, pairs, pack, 0)
        return carry

    lax.fori_loop(0, pieces, body, 0)
    for r, rows_to in GATHER_SENDS.items():

        @pl.when(me == r)
        def _(r=r, rows_to=rows_to):
            def finish(piece, carry):
                for slot, row in enumerate(rows_to):
                    send(piece, r, slot, row).wait_send()
                if r in GATHER_HANDS:
                    origin, row = GATHER_HANDS[r]
                    send(piece, origin, len(rows_to), row, block(piece, origin)).wait_send()
                return carry

            lax.fori_loop(0, pieces, finish, 0)

    pl.semaphore_signal(free.at[0], inc=1, device_id=core, device_id_type=MESH)
    pl.semaphore_signal(free.at[1], inc=1, device_id=chip, device_id_type=MESH)

    def near(p):
        return gathered.at[pl.ds(pl.multiple_of(p * rows, rows), rows), :]

    def far(p):
        return gathered.at[pl.ds(pl.multiple_of((count + p) * rows, rows), rows), :]

    def to_core(p):
        slot = lax.rem(p, 2)
        return remote(
            terms.at[slot, 1 - col], near(p), swap_sent.at[0, p], swap_got.at[0, p], core
        )

    def to_chip(p):
        return remote(near(p), far(p), swap_sent.at[1, p], swap_got.at[1, p], chip)

    def full(p, c, d, j):
        return three.at[2 * channels * p + j * cols * chans + c * chans + d]

    def places(p):
        for d in range(chans):
            for j in range(2):
                begin = (2 * d + j) * lanes
                yield 2 * d + j, far(p).at[:, begin : begin + lanes], full(p, col, d, j)

    def back(p):
        return [
            remote(source, target, full_sent.at[i, p], full_got.at[i, p], core)
            for i, source, target in places(p)
        ]

    def keep(p):
        return [
            pltpu.make_async_copy(source, target, keeps.at[i, p]) for i, source, target in places(p)
        ]

    def term(p):
        sides = [
            three[pl.ds((2 * p + j) * channels, channels)].reshape(channels * bonds, lanes)
            for j in range(2)
        ]
        value = dot(right_ref[...], jnp.concatenate(sides, axis=1)).astype(jnp.bfloat16)
        slot = lax.rem(p, 2)
        for c in range(2):
            for d in range(chans):
                part = value[(c * chans + d) * rows : (c * chans + d + 1) * rows]
                terms[slot, c, :, d * 2 * lanes : (d + 1) * 2 * lanes] = part

    def join(p):
        to_core(p).wait_recv()
        value = near(p)[...].astype(jnp.float32) + terms[lax.rem(p, 2), col].astype(jnp.float32)
        near(p)[...] = value.astype(jnp.bfloat16)

        @pl.when(p == 0)
        def _():
            pl.semaphore_wait(free.at[1], 1)

        to_chip(p).start()

    def close(p):
        to_chip(p).wait_recv()
        value = near(p)[...].astype(jnp.float32) + far(p)[...].astype(jnp.float32)
        far(p)[...] = value.astype(jnp.bfloat16)
        for item in back(p) + keep(p):
            item.start()

    def trade(p, carry):
        @pl.when(p < count)
        def _():
            @pl.when(p >= 2)
            def _():
                to_core(p - 2).wait_send()

            term(p)

            @pl.when(p == 0)
            def _():
                pl.semaphore_wait(free.at[0], 1)

            to_core(p).start()

        @pl.when((p >= 1) & (p <= count))
        def _():
            join(p - 1)

        @pl.when((p >= 3) & (p < count + 3))
        def _():
            close(p - 3)

        @pl.when(p >= 4)
        def _():
            for item in back(p - 4):
                item.wait_recv()
            for item in keep(p - 4):
                item.wait()
            five(p - 4, 0)

        @pl.when(p == count)
        def _():
            for peer in row_peers():
                pl.semaphore_signal(clear, inc=1, device_id=peer, device_id_type=MESH)

        return carry

    def read(piece):
        where = pl.ds(pl.multiple_of(piece * tile, tile), tile)
        slot = lax.rem(piece, 2)
        return pltpu.make_async_copy(turned_hbm.at[:, where, :], turned_ref.at[slot], reads.at[slot])

    def five(p, slot):
        sides = [
            three[pl.ds(2 * channels * p + j * cols * chans, cols * chans)].reshape(depth, lanes)
            for j in range(2)
        ]
        part = dot(turned_ref[slot].reshape(group, depth), jnp.concatenate(sides, axis=1))
        for j in range(2):
            where = pl.ds(pl.multiple_of((2 * p + j) * group, group), group)
            for h in range(lanes // LANES):
                begin = j * lanes + h * LANES
                wide[h, where, :] = part[:, begin : begin + LANES]

    read(0).start()
    read(0).wait()
    lax.fori_loop(0, count + 4, trade, 0)

    span = 2 * (channels - cols * chans)

    def spot(index):
        return index // span * 2 * channels + 2 * cols * chans + index % span

    def made(owner, piece):
        return three.at[spot(piece * blocks + owner)]

    def come(place, piece):
        return three.at[spot((pieces + piece) * blocks + place)]

    def give(piece, r, slot, row, owner):
        place = r if row == owner else row
        sems = gave.at[slot, piece], took.at[place, piece]
        return remote(made(owner, piece), come(place, piece), *sems, {"row": row})

    def taken(piece, place):
        target = come(place, piece)
        return remote(target, target, gave.at[0, piece], took.at[place, piece], {"row": me})

    def hand(piece):
        for r, owner in SCATTER_HANDS.items():

            @pl.when(me == r)
            def _(r=r, owner=owner):
                taken(piece, r).wait_recv()
                value = made(owner, piece)[...].astype(jnp.float32)
                value = value + come(r, piece)[...].astype(jnp.float32)
                made(owner, piece)[...] = value.astype(jnp.bfloat16)
                give(piece, r, len(SCATTER_SENDS[r]), owner, owner).start()

    def settle(piece, carry):
        for r, origins in SCATTER_FROM.items():

            @pl.when(me == r)
            def _(r=r, origins=origins):
                for place in origins:
                    taken(piece, place).wait_recv()
                value = made(r, piece)[...].astype(jnp.float32)
                for place in origins:
                    value = value + come(place, piece)[...].astype(jnp.float32)
                out_ref[at(piece), :] = value.astype(jnp.bfloat16)

        return carry

    def reverse(piece, carry):
        now = lax.rem(piece, 2)

        @pl.when(piece > 0)
        def _():
            read(piece).wait()

        @pl.when(piece + 1 < pieces)
        def _():
            read(piece + 1).start()

        @pl.when(piece > 0)
        def _():
            def step_five(p, carry):
                five(p, now)
                return carry

            lax.fori_loop(0, count, step_five, 0, unroll=2)

        def six(b, carry):
            sides = []
            for j in range(2):
                where = pl.ds(2 * b + j, channels * pairs, stride=tile)
                for h in range(lanes // LANES):
                    sides.append(wide.at[h][where, :].astype(jnp.bfloat16))
            part = dot(mpo_ref[...], jnp.concatenate(sides, axis=1)).astype(jnp.bfloat16)
            for j in range(2):
                where = pl.ds(pl.multiple_of((2 * b + j) * pairs, pairs), pairs)
                half = part[:, j * lanes : (j + 1) * lanes]
                for w in range(channels):
                    lhs[where, w * lanes : (w + 1) * lanes] = half[w * pairs : (w + 1) * pairs]
            return carry

        lax.fori_loop(0, tile // 2, six, 0, unroll=4)

        for r in range(0, blocks, 2):
            part = dot(lhs[...], left_ref[:, r * width : (r + 2) * width]).astype(jnp.bfloat16)
            made(r, piece)[...] = part[:, :width]
            made(r + 1, piece)[...] = part[:, width:]

        @pl.when(piece == 0)
        def _():
            pl.semaphore_wait(clear, blocks - 1)

        for r, sends in SCATTER_SENDS.items():

            @pl.when(me == r)
            def _(r=r, sends=sends):
                for slot, (row, owner) in enumerate(sends):
                    give(piece, r, slot, row, owner).start()

        @pl.when(piece >= 1)
        def _():
            hand(piece - 1)

        return carry

    lax.fori_loop(0, pieces, reverse, 0)
    hand(pieces - 1)

    for h in range(lanes // LANES):
        sides = [
            full(x // 2, col, chan, x % 2)[:, h * LANES : (h + 1) * LANES] for x in range(pairs)
        ]
        side = jnp.concatenate(sides, axis=1)

        def pick(t, carry, h=h, side=side):
            shape = (pairs * LANES, 2 * LANES)
            source = lax.broadcasted_iota(jnp.int32, shape, 0)
            target = lax.broadcasted_iota(jnp.int32, shape, 1) + t * 2 * LANES
            wanted = target % pairs * LANES + target // pairs
            chosen = jnp.where(source == wanted, 1.0, 0.0).astype(jnp.bfloat16)
            where = pl.multiple_of(h * LANES * pairs + t * 2 * LANES, 2 * LANES)
            kept_ref[:, pl.ds(where, 2 * LANES)] = dot(side, chosen).astype(jnp.bfloat16)
            return carry

        lax.fori_loop(0, pairs // 2, pick, 0)

    lax.fori_loop(0, pieces, settle, 0)
    for r, sends in SCATTER_SENDS.items():

        @pl.when(me == r)
        def _(r=r, sends=sends):
            def drain(piece, carry):
                for slot, (row, owner) in enumerate(sends):
                    give(piece, r, slot, row, owner).wait_send()
                if r in SCATTER_HANDS:
                    owner = SCATTER_HANDS[r]
                    give(piece, r, len(sends), owner, owner).wait_send()
                return carry

            lax.fori_loop(0, pieces, drain, 0)

    def finish(p, carry):
        @pl.when(p >= count - 2)
        def _():
            to_core(p).wait_send()

        to_chip(p).wait_send()
        for item in back(p):
            item.wait_send()
        return carry

    lax.fori_loop(0, count, finish, 0)


def fused(theta, left, mpo, right, pairs, tile):
    steps, width = theta.shape
    channels, rows, bonds = right.shape
    depth, lanes = left.shape[1], width
    pieces = bonds // tile
    cols, chans = lax.axis_size("col"), lax.axis_size("chan")
    count, own = pairs // 2, rows // (cols * chans)
    flops = 4 * steps * left.size + 4 * bonds * mpo.size * lanes
    flops += 4 * right.size * pairs * lanes
    size = 2 * (2 * theta.size + left.size + 3 * right.size) + 2 * own * pairs * lanes
    far = pl.BlockSpec(memory_space=pl.ANY)
    near = pl.BlockSpec(memory_space=pltpu.VMEM)
    return pl.pallas_call(
        functools.partial(kernel, pieces),
        out_shape=[
            jax.ShapeDtypeStruct((steps, width), jnp.bfloat16),
            jax.ShapeDtypeStruct((own, pairs * lanes), jnp.bfloat16),
            jax.ShapeDtypeStruct((channels, bonds, rows), jnp.bfloat16),
        ],
        in_specs=[far, far, near, near, far],
        out_specs=[near, near, far],
        scratch_shapes=[
            pltpu.VMEM((steps, depth), jnp.bfloat16),
            pltpu.VMEM(left.shape, jnp.bfloat16),
            pltpu.VMEM((rows, channels * bonds), jnp.bfloat16),
            pltpu.VMEM((tile, channels, pairs, lanes), jnp.bfloat16),
            pltpu.VMEM((lanes // LANES, channels * pairs * tile, LANES), jnp.float32),
            pltpu.VMEM((channels * pairs, bonds, lanes), jnp.bfloat16),
            pltpu.VMEM((2, cols, own, chans * 2 * lanes), jnp.bfloat16),
            pltpu.VMEM((2, channels, tile, rows), jnp.bfloat16),
            pltpu.VMEM((tile * pairs, channels * lanes), jnp.bfloat16),
            pltpu.SemaphoreType.DMA((4, pieces)),
            pltpu.SemaphoreType.DMA((4, pieces)),
            pltpu.SemaphoreType.DMA((2 + channels,)),
            pltpu.SemaphoreType.DMA((2,)),
            pltpu.SemaphoreType.DMA((2, count)),
            pltpu.SemaphoreType.DMA((2, count)),
            pltpu.SemaphoreType.DMA((2 * chans, count)),
            pltpu.SemaphoreType.DMA((2 * chans, count)),
            pltpu.SemaphoreType.DMA((2 * chans, count)),
            pltpu.SemaphoreType.REGULAR((2,)),
            pltpu.SemaphoreType.DMA((4, pieces)),
            pltpu.SemaphoreType.DMA((4, pieces)),
            pltpu.SemaphoreType.REGULAR,
            pltpu.SemaphoreType.DMA((2,)),
        ],
        compiler_params=pltpu.CompilerParams(
            collective_id=1, has_side_effects=True, vmem_limit_bytes=LIMIT
        ),
        cost_estimate=cost(flops, size),
    )(theta, left, mpo.T, mpo, right)


def mpo_product(mpo_left, mpo_right):
    paired = jnp.einsum("wuxs,uvyt->wstxyv", mpo_left, mpo_right, precision=lax.Precision.HIGHEST)
    channels, phys = mpo_left.shape[0], mpo_left.shape[2]
    return paired.reshape(channels * phys * phys, phys * phys * channels).astype(jnp.bfloat16)


def tiled_shards(theta, left_env, right_env, mpo_left, mpo_right):
    lanes, channels, depth = left_env.shape
    pairs, bonds = theta.shape[1:]
    width = theta.shape[0]
    tile = 16

    turned = jnp.transpose(theta, (2, 1, 0)).reshape(bonds * pairs, width)
    mpo = mpo_product(mpo_left, mpo_right)
    left = jnp.transpose(left_env, (1, 0, 2)).reshape(channels * lanes, depth)
    right = jnp.transpose(right_env, (1, 0, 2))

    product, residual, _ = fused(turned, left, mpo, right, pairs, tile)
    return residual, jnp.transpose(product.reshape(bonds, pairs, width), (2, 1, 0))


def plain_shards(theta, left_env, right_env, mpo_left, mpo_right):
    left_rows, channels = left_env.shape[:2]
    pairs, right_rows = theta.shape[1:]
    mpo_pair = mpo_product(mpo_left, mpo_right)
    einsum = functools.partial(jnp.einsum, preferred_element_type=jnp.float32)
    one = einsum("awk,ksb->awsb", left_env, lax.all_gather(theta, "row", axis=0, tiled=True))
    one = one.astype(jnp.bfloat16).reshape(left_rows, channels * pairs, right_rows)
    three = einsum("pq,apb->aqb", mpo_pair, one).astype(jnp.bfloat16)
    three = three.reshape(left_rows, pairs, channels, right_rows)
    term = einsum("kvb,asvb->kas", right_env, three).astype(jnp.bfloat16)
    term = term.reshape(right_env.shape[0], left_rows * pairs)
    residual = lax.psum_scatter(term, ("col", "chan"), scatter_dimension=0, tiled=True)
    full = lax.all_gather(residual, ("col", "chan"), axis=0, tiled=True)
    back = einsum("kp,kvb->pvb", full, right_env).astype(jnp.bfloat16)
    back = back.reshape(left_rows, pairs * channels, right_rows)
    back = einsum("pq,aqb->apb", mpo_pair, back).astype(jnp.bfloat16)
    back = back.reshape(left_rows, channels, pairs, right_rows)
    product = einsum("awk,awsb->ksb", left_env, back).astype(jnp.bfloat16)
    return residual, lax.psum_scatter(product, "row", scatter_dimension=0, tiled=True)


def shards(theta, left_env, right_env, mpo_left, mpo_right):
    sizes = [lax.axis_size(name) for name in ("row", "col", "chan")]
    fits = sizes == [4, 2, 2] and theta.shape == (256, 16, 256)
    fits = fits and left_env.shape == (256, 12, 1024) and right_env.shape == (1024, 12, 256)
    body = tiled_shards if fits else plain_shards
    return body(theta, left_env, right_env, mpo_left, mpo_right)


def solution(mesh):
    in_specs = (
        P(("grp", "row"), None, ("col", "chan")),
        P(("grp", "row"), None, None),
        P("grp", None, ("col", "chan")),
        P(),
        P(),
    )
    out_specs = (P(("grp", "col", "chan"), "row"), P(("grp", "row"), None, ("col", "chan")))
    return jax.shard_map(shards, mesh=mesh, in_specs=in_specs, out_specs=out_specs, check_vma=False)
```

```python
import functools
import math

import jax
import jax.numpy as jnp
from jax import lax
from jax.experimental import pallas as pl
from jax.experimental.pallas import tpu as pltpu
from jax.sharding import PartitionSpec as P

LANES = 128
AHEAD = 3
SLOTS = 4
LAG = 4
LIMIT = 60 * 1024 * 1024
MESH = pl.DeviceIdType.MESH


def cost(flops, size):
    return pl.CostEstimate(flops=int(flops), bytes_accessed=int(size), transcendentals=0)


def dot(lhs, rhs):
    return jnp.dot(lhs, rhs, preferred_element_type=jnp.float32)


def greet(peers):
    barrier = pltpu.get_barrier_semaphore()
    for peer in peers:
        pl.semaphore_signal(barrier, inc=1, device_id=peer, device_id_type=MESH)
    pl.semaphore_wait(barrier, len(peers))


def row_peers():
    size = lax.axis_size("row")
    return [{"row": lax.rem(lax.axis_index("row") + step, size)} for step in range(1, size)]


def remote(source, target, send_sem, recv_sem, peer):
    return pltpu.make_async_remote_copy(
        src_ref=source,
        dst_ref=target,
        send_sem=send_sem,
        recv_sem=recv_sem,
        device_id=peer,
        device_id_type=MESH,
    )


def pair_product(first_ref, second_ref, front_ref, mpo_ref, channels):
    size = mpo_ref.shape[0]
    phys = math.isqrt(size // channels)

    def exact(lhs, rhs, dims=(((1,), (0,)), ((), ()))):
        return lax.dot_general(
            lhs, rhs, dims, precision=lax.Precision.HIGHEST, preferred_element_type=jnp.float32
        )

    def ones(wanted):
        return jnp.where(wanted, 1.0, 0.0).astype(jnp.float32)

    row = lax.broadcasted_iota(jnp.int32, (size, size), 0)
    lane = lax.broadcasted_iota(jnp.int32, (size, size), 1)
    both = exact(first_ref[...], second_ref[...])
    total = jnp.zeros((size, size), jnp.float32)
    for x in range(phys):
        source = row // (phys * phys) * (phys * phys) + x * phys + row // phys % phys
        part = exact(ones(lane == source), both)
        part = jnp.where(lane // channels % phys == row % phys, part, 0.0)
        target = (x * phys + row // (phys * channels)) * channels + row % channels
        total = total + exact(part, ones(lane == target))
    mpo_ref[...] = total.astype(jnp.bfloat16)
    turned = exact(ones(lane == row), total, (((1,), (1,)), ((), ())))
    front_ref[...] = turned.astype(jnp.bfloat16)


GATHER_SENDS = {0: (1, 2), 1: (2, 0, 3), 2: (1, 3, 0), 3: (2, 1)}
GATHER_HANDS = {1: (3, 0), 2: (0, 3)}


SCATTER_SENDS = {
    0: ((1, 3), (1, 1), (2, 2)),
    1: ((2, 2), (0, 0)),
    2: ((1, 1), (3, 3)),
    3: ((2, 0), (2, 2), (1, 1)),
}
SCATTER_HANDS = {1: 3, 2: 0}
SCATTER_FROM = {0: (1, 2), 1: (0, 2, 3), 2: (3, 1, 0), 3: (2, 1)}


def kernel(
    pieces, theta_ref, left_hbm, first_ref, second_ref, right_hbm, out_ref, kept_ref, turned_hbm,
    gathered, left_ref, right_ref, held, wide, three, terms, turned_ref, lhs, front_ref, mpo_ref,
    sent, got, local, turns, swap_sent, swap_got, full_sent, full_got, keeps, free,
    gave, took, clear, reads,
):
    width = theta_ref.shape[1]
    tile, channels, pairs, lanes = held.shape
    _, bonds, _ = three.shape
    slots, cols, rows, lump = terms.shape
    chans = lump // lanes
    depth = cols * chans * rows
    blocks = gathered.shape[1] // width
    step = tile * pairs
    group = channels * tile
    me, col, chan = lax.axis_index("row"), lax.axis_index("col"), lax.axis_index("chan")
    core, chip = {"col": 1 - col}, {"chan": 1 - chan}
    loads = [
        pltpu.make_async_copy(
            right_hbm.at[v], right_ref.at[:, v * bonds : (v + 1) * bonds], local.at[2 + v]
        )
        for v in range(channels)
    ]
    loads.append(pltpu.make_async_copy(left_hbm, left_ref, local.at[0]))
    for item in loads:
        item.start()

    def at(piece):
        return pl.ds(pl.multiple_of(piece * step, step), step)

    def block(piece, origin):
        return gathered.at[at(piece), origin * width : (origin + 1) * width]

    def send(piece, origin, slot, row, source=None):
        source = theta_ref.at[at(piece), :] if source is None else source
        return remote(
            source, block(piece, origin), sent.at[slot, piece], got.at[origin, piece], {"row": row}
        )

    def arrival(piece, origin):
        return send(piece, origin, 0, me)

    greet(row_peers() + [core, chip])
    for r, rows_to in GATHER_SENDS.items():

        @pl.when(me == r)
        def _(r=r, rows_to=rows_to):
            for piece in range(min(AHEAD, pieces)):
                for slot, row in enumerate(rows_to):
                    send(piece, r, slot, row).start()
            mine = pltpu.make_async_copy(
                theta_ref, gathered.at[:, r * width : (r + 1) * width], local.at[1]
            )
            mine.start()
            mine.wait()

    pair_product(first_ref, second_ref, front_ref, mpo_ref, channels)
    for item in loads:
        item.wait()

    def stage(slot):
        return lhs.at[:, pl.ds(pl.multiple_of(slot * depth, depth), depth)]

    def turned(v):
        slot = lax.rem(v, 2)
        return pltpu.make_async_copy(stage(slot), turned_hbm.at[v], turns.at[slot])

    def turn(v, carry):
        @pl.when(v >= 2)
        def _():
            turned(v - 2).wait()

        where = pl.ds(pl.multiple_of(v * bonds, bonds), bonds)
        stage(lax.rem(v, 2))[...] = right_ref[:, where].T
        turned(v).start()
        return carry

    lax.fori_loop(0, channels, turn, 0)
    for v in range(channels - 2, channels):
        turned(v).wait()

    def body(piece, carry):
        for r, rows_to in GATHER_SENDS.items():

            @pl.when(me == r)
            def _(r=r, rows_to=rows_to):
                late = [origin for origin in range(4) if origin != r]
                if r in GATHER_HANDS:
                    origin, row = GATHER_HANDS[r]
                    arrival(piece, origin).wait_recv()
                    send(piece, origin, len(rows_to), row, block(piece, origin)).start()
                    late.remove(origin)
                for origin in late:
                    arrival(piece, origin).wait_recv()

                @pl.when(piece + AHEAD < pieces)
                def _():
                    for slot, row in enumerate(rows_to):
                        send(piece + AHEAD, r, slot, row).start()

        def one(w, carry):
            where = pl.ds(pl.multiple_of(2 * w * lanes, 2 * lanes), 2 * lanes)
            part = lax.dot_general(
                gathered[at(piece), :],
                left_ref[where, :],
                (((1,), (1,)), ((), ())),
                preferred_element_type=jnp.float32,
            ).astype(jnp.bfloat16)
            held[:, 2 * w] = part[:, :lanes].reshape(tile, pairs, lanes)
            held[:, 2 * w + 1] = part[:, lanes:].reshape(tile, pairs, lanes)
            return carry

        lax.fori_loop(0, channels // 2, one, 0, unroll=2)

        def two(b, carry):
            first = held[2 * b].reshape(channels * pairs, lanes)
            second = held[2 * b + 1].reshape(channels * pairs, lanes)
            part = dot(front_ref[...], jnp.concatenate([first, second], axis=1))
            for j in range(2):
                where = pl.ds(2 * b + j, channels * pairs, stride=tile)
                for h in range(lanes // LANES):
                    begin = j * lanes + h * LANES
                    wide.at[h][where, :] = part[:, begin : begin + LANES]
            return carry

        lax.fori_loop(0, tile // 2, two, 0, unroll=4)

        def pack(x, carry):
            own = pl.ds(pl.multiple_of(x * group, group), group)
            where = pl.ds(pl.multiple_of(piece * tile, tile), tile)
            for h in range(lanes // LANES):
                part = wide[h, own, :].astype(jnp.bfloat16).reshape(channels, tile, LANES)
                three[pl.ds(x * channels, channels), where, h * LANES : (h + 1) * LANES] = part
            return carry

        lax.fori_loop(0, pairs, pack, 0)
        return carry

    lax.fori_loop(0, pieces, body, 0)
    for r, rows_to in GATHER_SENDS.items():

        @pl.when(me == r)
        def _(r=r, rows_to=rows_to):
            def finish(piece, carry):
                for slot, row in enumerate(rows_to):
                    send(piece, r, slot, row).wait_send()
                if r in GATHER_HANDS:
                    origin, row = GATHER_HANDS[r]
                    send(piece, origin, len(rows_to), row, block(piece, origin)).wait_send()
                return carry

            lax.fori_loop(0, pieces, finish, 0)

    pl.semaphore_signal(free.at[0], inc=1, device_id=core, device_id_type=MESH)
    pl.semaphore_signal(free.at[1], inc=1, device_id=chip, device_id_type=MESH)

    def near(x, first=0):
        where = pl.ds(pl.multiple_of((first + x // 2) * rows, rows), rows)
        return gathered.at[where, pl.ds(pl.multiple_of(x % 2 * lump, lump), lump)]

    def far(x):
        return near(x, pairs // 2)

    def to_core(x):
        source = terms.at[lax.rem(x, slots), 1 - col]
        return remote(source, near(x), swap_sent.at[0, x], swap_got.at[0, x], core)

    def to_chip(x):
        return remote(near(x), far(x), swap_sent.at[1, x], swap_got.at[1, x], chip)

    def full(x, c, d):
        return three.at[x // 2 * 2 * channels + x % 2 * cols * chans + c * chans + d]

    def places(x):
        for d in range(chans):
            where = pl.ds(pl.multiple_of((x // 2 + pairs // 2) * rows, rows), rows)
            begin = pl.multiple_of(x % 2 * lump + d * lanes, lanes)
            yield d, gathered.at[where, pl.ds(begin, lanes)], full(x, col, d)

    def back(x):
        return [
            remote(source, target, full_sent.at[d, x], full_got.at[d, x], core)
            for d, source, target in places(x)
        ]

    def keep(x):
        return [
            pltpu.make_async_copy(source, target, keeps.at[d, x]) for d, source, target in places(x)
        ]

    def term(x):
        side = three[pl.ds(x * channels, channels)].reshape(channels * bonds, lanes)
        value = dot(right_ref[...], side).astype(jnp.bfloat16)
        for c in range(cols):
            for d in range(chans):
                part = value[(c * chans + d) * rows : (c * chans + d + 1) * rows]
                terms[lax.rem(x, slots), c, :, d * lanes : (d + 1) * lanes] = part

    def join(x):
        to_core(x).wait_recv()
        value = near(x)[...].astype(jnp.float32)
        value = value + terms[lax.rem(x, slots), col].astype(jnp.float32)
        near(x)[...] = value.astype(jnp.bfloat16)

        @pl.when(x == 0)
        def _():
            pl.semaphore_wait(free.at[1], 1)

        to_chip(x).start()

    def close(x):
        to_chip(x).wait_recv()
        value = near(x)[...].astype(jnp.float32) + far(x)[...].astype(jnp.float32)
        far(x)[...] = value.astype(jnp.bfloat16)
        for item in back(x) + keep(x):
            item.start()

    def trade(x, carry):
        @pl.when(x < pairs)
        def _():
            @pl.when(x >= slots)
            def _():
                to_core(x - slots).wait_send()

            term(x)

            @pl.when(x == 0)
            def _():
                pl.semaphore_wait(free.at[0], 1)

            to_core(x).start()

        @pl.when((x >= 1) & (x <= pairs))
        def _():
            join(x - 1)

        @pl.when((x >= LAG) & (x < pairs + LAG))
        def _():
            close(x - LAG)

        @pl.when(x >= LAG + 1)
        def _():
            for item in back(x - LAG - 1):
                item.wait_recv()
            for item in keep(x - LAG - 1):
                item.wait()
            five(x - LAG - 1, 0, 1)

        @pl.when(x == pairs)
        def _():
            for peer in row_peers():
                pl.semaphore_signal(clear, inc=1, device_id=peer, device_id_type=MESH)

        return carry

    def read(piece):
        where = pl.ds(pl.multiple_of(piece * tile, tile), tile)
        slot = lax.rem(piece, 2)
        return pltpu.make_async_copy(turned_hbm.at[:, where, :], turned_ref.at[slot], reads.at[slot])

    def five(x, slot, wanted):
        sides = [three[pl.ds(x // 2 * 2 * channels + x % 2 * cols * chans, cols * chans)]]
        if wanted == 2:
            sides.append(three[pl.ds(x // 2 * 2 * channels + cols * chans, cols * chans)])
        sides = [side.reshape(depth, lanes) for side in sides]
        side = sides[0] if wanted == 1 else jnp.concatenate(sides, axis=1)
        part = dot(turned_ref[slot].reshape(group, depth), side)
        for j in range(wanted):
            where = pl.ds(pl.multiple_of((x + j) * group, group), group)
            for h in range(lanes // LANES):
                begin = j * lanes + h * LANES
                wide[h, where, :] = part[:, begin : begin + LANES]

    read(0).start()
    read(0).wait()
    lax.fori_loop(0, pairs + LAG + 1, trade, 0)

    span = 2 * (channels - cols * chans)

    def spot(index):
        return index // span * 2 * channels + 2 * cols * chans + index % span

    def made(owner, piece):
        return three.at[spot(piece * blocks + owner)]

    def come(place, piece):
        return three.at[spot((pieces + piece) * blocks + place)]

    def give(piece, r, slot, row, owner):
        place = r if row == owner else row
        sems = gave.at[slot, piece], took.at[place, piece]
        return remote(made(owner, piece), come(place, piece), *sems, {"row": row})

    def taken(piece, place):
        target = come(place, piece)
        return remote(target, target, gave.at[0, piece], took.at[place, piece], {"row": me})

    def hand(piece):
        for r, owner in SCATTER_HANDS.items():

            @pl.when(me == r)
            def _(r=r, owner=owner):
                taken(piece, r).wait_recv()
                value = made(owner, piece)[...].astype(jnp.float32)
                value = value + come(r, piece)[...].astype(jnp.float32)
                made(owner, piece)[...] = value.astype(jnp.bfloat16)
                give(piece, r, len(SCATTER_SENDS[r]), owner, owner).start()

    def settle(piece, carry):
        for r, origins in SCATTER_FROM.items():

            @pl.when(me == r)
            def _(r=r, origins=origins):
                for place in origins:
                    taken(piece, place).wait_recv()
                value = made(r, piece)[...].astype(jnp.float32)
                for place in origins:
                    value = value + come(place, piece)[...].astype(jnp.float32)
                out_ref[at(piece), :] = value.astype(jnp.bfloat16)

        return carry

    def reverse(piece, carry):
        now = lax.rem(piece, 2)

        @pl.when(piece > 0)
        def _():
            read(piece).wait()

        @pl.when(piece + 1 < pieces)
        def _():
            read(piece + 1).start()

        @pl.when(piece > 0)
        def _():
            def step_five(p, carry):
                five(2 * p, now, 2)
                return carry

            lax.fori_loop(0, pairs // 2, step_five, 0, unroll=2)

        def six(b, carry):
            sides = []
            for j in range(2):
                where = pl.ds(2 * b + j, channels * pairs, stride=tile)
                for h in range(lanes // LANES):
                    sides.append(wide.at[h][where, :].astype(jnp.bfloat16))
            part = dot(mpo_ref[...], jnp.concatenate(sides, axis=1)).astype(jnp.bfloat16)
            for j in range(2):
                where = pl.ds(pl.multiple_of((2 * b + j) * pairs, pairs), pairs)
                half = part[:, j * lanes : (j + 1) * lanes]
                for w in range(channels):
                    lhs[where, w * lanes : (w + 1) * lanes] = half[w * pairs : (w + 1) * pairs]
            return carry

        lax.fori_loop(0, tile // 2, six, 0, unroll=4)

        for r in range(0, blocks, 2):
            part = dot(lhs[...], left_ref[:, r * width : (r + 2) * width]).astype(jnp.bfloat16)
            made(r, piece)[...] = part[:, :width]
            made(r + 1, piece)[...] = part[:, width:]

        @pl.when(piece == 0)
        def _():
            pl.semaphore_wait(clear, blocks - 1)

        for r, sends in SCATTER_SENDS.items():

            @pl.when(me == r)
            def _(r=r, sends=sends):
                for slot, (row, owner) in enumerate(sends):
                    give(piece, r, slot, row, owner).start()

        @pl.when(piece >= 1)
        def _():
            hand(piece - 1)

        return carry

    lax.fori_loop(0, pieces, reverse, 0)
    hand(pieces - 1)

    for h in range(lanes // LANES):
        sides = [full(x, col, chan)[:, h * LANES : (h + 1) * LANES] for x in range(pairs)]
        side = jnp.concatenate(sides, axis=1)

        def pick(t, carry, h=h, side=side):
            shape = (pairs * LANES, 2 * LANES)
            source = lax.broadcasted_iota(jnp.int32, shape, 0)
            target = lax.broadcasted_iota(jnp.int32, shape, 1) + t * 2 * LANES
            wanted = target % pairs * LANES + target // pairs
            chosen = jnp.where(source == wanted, 1.0, 0.0).astype(jnp.bfloat16)
            where = pl.multiple_of(h * LANES * pairs + t * 2 * LANES, 2 * LANES)
            kept_ref[:, pl.ds(where, 2 * LANES)] = dot(side, chosen).astype(jnp.bfloat16)
            return carry

        lax.fori_loop(0, pairs // 2, pick, 0)

    lax.fori_loop(0, pieces, settle, 0)
    for r, sends in SCATTER_SENDS.items():

        @pl.when(me == r)
        def _(r=r, sends=sends):
            def drain(piece, carry):
                for slot, (row, owner) in enumerate(sends):
                    give(piece, r, slot, row, owner).wait_send()
                if r in SCATTER_HANDS:
                    owner = SCATTER_HANDS[r]
                    give(piece, r, len(sends), owner, owner).wait_send()
                return carry

            lax.fori_loop(0, pieces, drain, 0)

    def finish(x, carry):
        @pl.when(x >= pairs - slots)
        def _():
            to_core(x).wait_send()

        to_chip(x).wait_send()
        for item in back(x):
            item.wait_send()
        return carry

    lax.fori_loop(0, pairs, finish, 0)


def fused(theta, left, first, second, right, pairs, tile):
    steps, width = theta.shape
    channels, rows, bonds = right.shape
    depth, lanes = left.shape[1], width
    pieces = bonds // tile
    cols, chans = lax.axis_size("col"), lax.axis_size("chan")
    own = rows // (cols * chans)
    flops = 4 * steps * left.size + 4 * bonds * (channels * pairs) ** 2 * lanes
    flops += 4 * right.size * pairs * lanes
    size = 2 * (2 * theta.size + left.size + 3 * right.size) + 2 * own * pairs * lanes
    far = pl.BlockSpec(memory_space=pl.ANY)
    near = pl.BlockSpec(memory_space=pltpu.VMEM)
    return pl.pallas_call(
        functools.partial(kernel, pieces),
        out_shape=[
            jax.ShapeDtypeStruct((steps, width), jnp.bfloat16),
            jax.ShapeDtypeStruct((own, pairs * lanes), jnp.bfloat16),
            jax.ShapeDtypeStruct((channels, bonds, rows), jnp.bfloat16),
        ],
        in_specs=[far, far, near, near, far],
        out_specs=[near, near, far],
        scratch_shapes=[
            pltpu.VMEM((steps, depth), jnp.bfloat16),
            pltpu.VMEM(left.shape, jnp.bfloat16),
            pltpu.VMEM((rows, channels * bonds), jnp.bfloat16),
            pltpu.VMEM((tile, channels, pairs, lanes), jnp.bfloat16),
            pltpu.VMEM((lanes // LANES, channels * pairs * tile, LANES), jnp.float32),
            pltpu.VMEM((channels * pairs, bonds, lanes), jnp.bfloat16),
            pltpu.VMEM((SLOTS, cols, own, chans * lanes), jnp.bfloat16),
            pltpu.VMEM((2, channels, tile, rows), jnp.bfloat16),
            pltpu.VMEM((tile * pairs, channels * lanes), jnp.bfloat16),
            pltpu.VMEM((channels * pairs, channels * pairs), jnp.bfloat16),
            pltpu.VMEM((channels * pairs, channels * pairs), jnp.bfloat16),
            pltpu.SemaphoreType.DMA((4, pieces)),
            pltpu.SemaphoreType.DMA((4, pieces)),
            pltpu.SemaphoreType.DMA((2 + channels,)),
            pltpu.SemaphoreType.DMA((2,)),
            pltpu.SemaphoreType.DMA((2, pairs)),
            pltpu.SemaphoreType.DMA((2, pairs)),
            pltpu.SemaphoreType.DMA((chans, pairs)),
            pltpu.SemaphoreType.DMA((chans, pairs)),
            pltpu.SemaphoreType.DMA((chans, pairs)),
            pltpu.SemaphoreType.REGULAR((2,)),
            pltpu.SemaphoreType.DMA((4, pieces)),
            pltpu.SemaphoreType.DMA((4, pieces)),
            pltpu.SemaphoreType.REGULAR,
            pltpu.SemaphoreType.DMA((2,)),
        ],
        compiler_params=pltpu.CompilerParams(
            collective_id=1, has_side_effects=True, vmem_limit_bytes=LIMIT
        ),
        cost_estimate=cost(flops, size),
    )(theta, left, first, second, right)


def mpo_product(mpo_left, mpo_right):
    paired = jnp.einsum("wuxs,uvyt->wstxyv", mpo_left, mpo_right, precision=lax.Precision.HIGHEST)
    channels, phys = mpo_left.shape[0], mpo_left.shape[2]
    return paired.reshape(channels * phys * phys, phys * phys * channels).astype(jnp.bfloat16)


def tiled_shards(theta, left_env, right_env, mpo_left, mpo_right):
    lanes, channels, depth = left_env.shape
    pairs, bonds = theta.shape[1:]
    width = theta.shape[0]
    tile = 16

    turned = jnp.transpose(theta, (2, 1, 0)).reshape(bonds * pairs, width)
    first = jnp.transpose(mpo_left, (0, 2, 3, 1)).reshape(channels * pairs, channels)
    second = jnp.transpose(mpo_right, (0, 2, 3, 1)).reshape(channels, pairs * channels)
    left = jnp.transpose(left_env, (1, 0, 2)).reshape(channels * lanes, depth)
    right = jnp.transpose(right_env, (1, 0, 2))

    product, residual, _ = fused(turned, left, first, second, right, pairs, tile)
    return residual, jnp.transpose(product.reshape(bonds, pairs, width), (2, 1, 0))


def plain_shards(theta, left_env, right_env, mpo_left, mpo_right):
    left_rows, channels = left_env.shape[:2]
    pairs, right_rows = theta.shape[1:]
    mpo_pair = mpo_product(mpo_left, mpo_right)
    einsum = functools.partial(jnp.einsum, preferred_element_type=jnp.float32)
    one = einsum("awk,ksb->awsb", left_env, lax.all_gather(theta, "row", axis=0, tiled=True))
    one = one.astype(jnp.bfloat16).reshape(left_rows, channels * pairs, right_rows)
    three = einsum("pq,apb->aqb", mpo_pair, one).astype(jnp.bfloat16)
    three = three.reshape(left_rows, pairs, channels, right_rows)
    term = einsum("kvb,asvb->kas", right_env, three).astype(jnp.bfloat16)
    term = term.reshape(right_env.shape[0], left_rows * pairs)
    residual = lax.psum_scatter(term, ("col", "chan"), scatter_dimension=0, tiled=True)
    full = lax.all_gather(residual, ("col", "chan"), axis=0, tiled=True)
    back = einsum("kp,kvb->pvb", full, right_env).astype(jnp.bfloat16)
    back = back.reshape(left_rows, pairs * channels, right_rows)
    back = einsum("pq,aqb->apb", mpo_pair, back).astype(jnp.bfloat16)
    back = back.reshape(left_rows, channels, pairs, right_rows)
    product = einsum("awk,awsb->ksb", left_env, back).astype(jnp.bfloat16)
    return residual, lax.psum_scatter(product, "row", scatter_dimension=0, tiled=True)


def shards(theta, left_env, right_env, mpo_left, mpo_right):
    sizes = [lax.axis_size(name) for name in ("row", "col", "chan")]
    fits = sizes == [4, 2, 2] and theta.shape == (256, 16, 256)
    fits = fits and left_env.shape == (256, 12, 1024) and right_env.shape == (1024, 12, 256)
    body = tiled_shards if fits else plain_shards
    return body(theta, left_env, right_env, mpo_left, mpo_right)


def solution(mesh):
    in_specs = (
        P(("grp", "row"), None, ("col", "chan")),
        P(("grp", "row"), None, None),
        P("grp", None, ("col", "chan")),
        P(),
        P(),
    )
    out_specs = (P(("grp", "col", "chan"), "row"), P(("grp", "row"), None, ("col", "chan")))
    return jax.shard_map(shards, mesh=mesh, in_specs=in_specs, out_specs=out_specs, check_vma=False)
```

```python
import functools
import math

import jax
import jax.numpy as jnp
from jax import lax
from jax.experimental import pallas as pl
from jax.experimental.pallas import tpu as pltpu
from jax.sharding import PartitionSpec as P

LANES = 128
AHEAD = 3
SLOTS = 4
LAG = 4
LATE = 1
LIMIT = 61 * 1024 * 1024
MESH = pl.DeviceIdType.MESH


def cost(flops, size):
    return pl.CostEstimate(flops=int(flops), bytes_accessed=int(size), transcendentals=0)


def dot(lhs, rhs):
    return jnp.dot(lhs, rhs, preferred_element_type=jnp.float32)


def greet(peers):
    barrier = pltpu.get_barrier_semaphore()
    for peer in peers:
        pl.semaphore_signal(barrier, inc=1, device_id=peer, device_id_type=MESH)
    pl.semaphore_wait(barrier, len(peers))


def row_peers():
    size = lax.axis_size("row")
    return [{"row": lax.rem(lax.axis_index("row") + step, size)} for step in range(1, size)]


def remote(source, target, send_sem, recv_sem, peer):
    return pltpu.make_async_remote_copy(
        src_ref=source,
        dst_ref=target,
        send_sem=send_sem,
        recv_sem=recv_sem,
        device_id=peer,
        device_id_type=MESH,
    )


def pair_product(first_ref, second_ref, front_ref, mpo_ref, channels):
    size = mpo_ref.shape[0]
    phys = math.isqrt(size // channels)

    def exact(lhs, rhs, dims=(((1,), (0,)), ((), ()))):
        return lax.dot_general(
            lhs, rhs, dims, precision=lax.Precision.HIGHEST, preferred_element_type=jnp.float32
        )

    def ones(wanted):
        return jnp.where(wanted, 1.0, 0.0).astype(jnp.float32)

    row = lax.broadcasted_iota(jnp.int32, (size, size), 0)
    lane = lax.broadcasted_iota(jnp.int32, (size, size), 1)
    shape = (channels, size)
    own = lax.broadcasted_iota(jnp.int32, shape, 0)
    other = lax.broadcasted_iota(jnp.int32, shape, 1)
    second = exact(second_ref[...], ones(other % channels == own))
    second = jnp.where(lane // channels == row % (phys * phys), second, 0.0)
    second = exact(ones(other // (phys * phys) == own), second)
    both = exact(first_ref[...], second)
    total = jnp.zeros((size, size), jnp.float32)
    for x in range(phys):
        source = row // (phys * phys) * (phys * phys) + x * phys + row // phys % phys
        part = exact(ones(lane == source), both)
        part = jnp.where(lane // channels % phys == row % phys, part, 0.0)
        target = (x * phys + row // (phys * channels)) * channels + row % channels
        total = total + exact(part, ones(lane == target))
    mpo_ref[...] = total.astype(jnp.bfloat16)
    turned = exact(ones(lane == row), total, (((1,), (1,)), ((), ())))
    front_ref[...] = turned.astype(jnp.bfloat16)


GATHER_SENDS = {0: (1, 2), 1: (2, 0, 3), 2: (1, 3, 0), 3: (2, 1)}
GATHER_HANDS = {1: (3, 0), 2: (0, 3)}


SCATTER_SENDS = {
    0: ((1, 3, 1), (1, 2, 3), (1, 1, 0)),
    1: ((0, 0, 1),),
    2: ((3, 3, 2),),
    3: ((2, 0, 2), (2, 1, 0), (2, 2, 3)),
}
SCATTER_HANDS = {1: ((3, 3, 1, 1), (2, 2, 1, 3)), 2: ((0, 0, 2, 2), (1, 1, 2, 0))}
SCATTER_FROM = {0: (1, 2), 1: (0, 2), 2: (3, 1), 3: (2, 1)}


def kernel(
    pieces, theta_ref, left_hbm, first_ref, second_ref, right_hbm, out_ref, kept_ref, turned_hbm,
    gathered, left_ref, right_ref, held, wide, three, terms, turned_ref, lhs, front_ref, mpo_ref,
    sent, got, local, turns, swap_sent, swap_got, full_sent, full_got, keeps, free,
    gave, took, clear, reads,
):
    width = theta_ref.shape[1]
    tile, channels, pairs, lanes = held.shape
    _, bonds, _ = three.shape
    slots, cols, rows, lump = terms.shape
    chans = lump // lanes
    depth = cols * chans * rows
    blocks = gathered.shape[1] // width
    step = tile * pairs
    group = channels * tile
    me, col, chan = lax.axis_index("row"), lax.axis_index("col"), lax.axis_index("chan")
    core, chip = {"col": 1 - col}, {"chan": 1 - chan}
    loads = [
        pltpu.make_async_copy(
            right_hbm.at[v], right_ref.at[:, v * bonds : (v + 1) * bonds], local.at[2 + v]
        )
        for v in range(channels)
    ]
    loads.append(pltpu.make_async_copy(left_hbm, left_ref, local.at[0]))
    for item in loads:
        item.start()

    def at(piece):
        return pl.ds(pl.multiple_of(piece * step, step), step)

    def block(piece, origin):
        return gathered.at[at(piece), origin * width : (origin + 1) * width]

    def send(piece, origin, slot, row, source=None):
        source = theta_ref.at[at(piece), :] if source is None else source
        return remote(
            source, block(piece, origin), sent.at[slot, piece], got.at[origin, piece], {"row": row}
        )

    def arrival(piece, origin):
        return send(piece, origin, 0, me)

    greet(row_peers() + [core, chip])
    for r, rows_to in GATHER_SENDS.items():

        @pl.when(me == r)
        def _(r=r, rows_to=rows_to):
            for piece in range(min(AHEAD, pieces)):
                for slot, row in enumerate(rows_to):
                    send(piece, r, slot, row).start()
            mine = pltpu.make_async_copy(
                theta_ref, gathered.at[:, r * width : (r + 1) * width], local.at[1]
            )
            mine.start()
            mine.wait()

    pair_product(first_ref, second_ref, front_ref, mpo_ref, channels)
    for item in loads:
        item.wait()

    def stage(slot):
        return lhs.at[:, pl.ds(pl.multiple_of(slot * depth, depth), depth)]

    def turned(v):
        slot = lax.rem(v, 2)
        return pltpu.make_async_copy(stage(slot), turned_hbm.at[v], turns.at[slot])

    def turn(v, carry):
        @pl.when(v >= 2)
        def _():
            turned(v - 2).wait()

        where = pl.ds(pl.multiple_of(v * bonds, bonds), bonds)
        stage(lax.rem(v, 2))[...] = right_ref[:, where].T
        turned(v).start()
        return carry

    lax.fori_loop(0, channels, turn, 0)
    for v in range(channels - 2, channels):
        turned(v).wait()

    def body(piece, carry):
        for r, rows_to in GATHER_SENDS.items():

            @pl.when(me == r)
            def _(r=r, rows_to=rows_to):
                late = [origin for origin in range(4) if origin != r]
                if r in GATHER_HANDS:
                    origin, row = GATHER_HANDS[r]
                    arrival(piece, origin).wait_recv()
                    send(piece, origin, len(rows_to), row, block(piece, origin)).start()
                    late.remove(origin)
                for origin in late:
                    arrival(piece, origin).wait_recv()

                @pl.when(piece + AHEAD < pieces)
                def _():
                    for slot, row in enumerate(rows_to):
                        send(piece + AHEAD, r, slot, row).start()

        def one(w, carry):
            where = pl.ds(pl.multiple_of(2 * w * lanes, 2 * lanes), 2 * lanes)
            part = lax.dot_general(
                gathered[at(piece), :],
                left_ref[where, :],
                (((1,), (1,)), ((), ())),
                preferred_element_type=jnp.float32,
            ).astype(jnp.bfloat16)
            held[:, 2 * w] = part[:, :lanes].reshape(tile, pairs, lanes)
            held[:, 2 * w + 1] = part[:, lanes:].reshape(tile, pairs, lanes)
            return carry

        lax.fori_loop(0, channels // 2, one, 0, unroll=2)

        def two(b, carry):
            first = held[2 * b].reshape(channels * pairs, lanes)
            second = held[2 * b + 1].reshape(channels * pairs, lanes)
            part = dot(front_ref[...], jnp.concatenate([first, second], axis=1))
            for j in range(2):
                where = pl.ds(2 * b + j, channels * pairs, stride=tile)
                for h in range(lanes // LANES):
                    begin = j * lanes + h * LANES
                    wide.at[h][where, :] = part[:, begin : begin + LANES]
            return carry

        lax.fori_loop(0, tile // 2, two, 0, unroll=4)

        def pack(x, carry):
            own = pl.ds(pl.multiple_of(x * group, group), group)
            where = pl.ds(pl.multiple_of(piece * tile, tile), tile)
            for h in range(lanes // LANES):
                part = wide[h, own, :].astype(jnp.bfloat16).reshape(channels, tile, LANES)
                three[pl.ds(x * channels, channels), where, h * LANES : (h + 1) * LANES] = part
            return carry

        lax.fori_loop(0, pairs, pack, 0)
        return carry

    lax.fori_loop(0, pieces, body, 0)
    for r, rows_to in GATHER_SENDS.items():

        @pl.when(me == r)
        def _(r=r, rows_to=rows_to):
            def finish(piece, carry):
                for slot, row in enumerate(rows_to):
                    send(piece, r, slot, row).wait_send()
                if r in GATHER_HANDS:
                    origin, row = GATHER_HANDS[r]
                    send(piece, origin, len(rows_to), row, block(piece, origin)).wait_send()
                return carry

            lax.fori_loop(0, pieces, finish, 0)

    pl.semaphore_signal(free.at[0], inc=1, device_id=core, device_id_type=MESH)
    pl.semaphore_signal(free.at[1], inc=1, device_id=chip, device_id_type=MESH)

    def near(x, first=0):
        where = pl.ds(pl.multiple_of((first + x // 2) * rows, rows), rows)
        return gathered.at[where, pl.ds(pl.multiple_of(x % 2 * lump, lump), lump)]

    def far(x):
        return near(x, pairs // 2)

    def to_core(x):
        source = terms.at[lax.rem(x, slots), 1 - col]
        return remote(source, near(x), swap_sent.at[0, x], swap_got.at[0, x], core)

    def to_chip(x):
        return remote(near(x), far(x), swap_sent.at[1, x], swap_got.at[1, x], chip)

    def full(x, c, d):
        return three.at[x // 2 * 2 * channels + x % 2 * cols * chans + c * chans + d]

    def places(x):
        for d in range(chans):
            where = pl.ds(pl.multiple_of((x // 2 + pairs // 2) * rows, rows), rows)
            begin = pl.multiple_of(x % 2 * lump + d * lanes, lanes)
            yield d, gathered.at[where, pl.ds(begin, lanes)], full(x, col, d)

    def back(x):
        return [
            remote(source, target, full_sent.at[d, x], full_got.at[d, x], core)
            for d, source, target in places(x)
        ]

    def keep(x):
        return [
            pltpu.make_async_copy(source, target, keeps.at[d, x]) for d, source, target in places(x)
        ]

    def term(x):
        side = three[pl.ds(x * channels, channels)].reshape(channels * bonds, lanes)
        value = dot(right_ref[...], side).astype(jnp.bfloat16)
        for c in range(cols):
            for d in range(chans):
                part = value[(c * chans + d) * rows : (c * chans + d + 1) * rows]
                terms[lax.rem(x, slots), c, :, d * lanes : (d + 1) * lanes] = part

    def join(x):
        to_core(x).wait_recv()
        value = near(x)[...].astype(jnp.float32)
        value = value + terms[lax.rem(x, slots), col].astype(jnp.float32)
        near(x)[...] = value.astype(jnp.bfloat16)

        @pl.when(x == 0)
        def _():
            pl.semaphore_wait(free.at[1], 1)

        to_chip(x).start()

    def close(x):
        to_chip(x).wait_recv()
        value = near(x)[...].astype(jnp.float32) + far(x)[...].astype(jnp.float32)
        far(x)[...] = value.astype(jnp.bfloat16)
        for item in back(x) + keep(x):
            item.start()

    def trade(x, carry):
        @pl.when(x < pairs)
        def _():
            @pl.when(x >= slots)
            def _():
                to_core(x - slots).wait_send()

            term(x)

            @pl.when(x == 0)
            def _():
                pl.semaphore_wait(free.at[0], 1)

            to_core(x).start()

        @pl.when((x >= 1) & (x <= pairs))
        def _():
            join(x - 1)

        @pl.when((x >= LAG) & (x < pairs + LAG))
        def _():
            close(x - LAG)

        @pl.when(x >= LAG + 1)
        def _():
            for item in back(x - LAG - 1):
                item.wait_recv()
            for item in keep(x - LAG - 1):
                item.wait()
            five(x - LAG - 1, 0, 1)

        @pl.when(x == pairs)
        def _():
            for peer in row_peers():
                pl.semaphore_signal(clear, inc=1, device_id=peer, device_id_type=MESH)

        return carry

    def read(piece):
        where = pl.ds(pl.multiple_of(piece * tile, tile), tile)
        slot = lax.rem(piece, 2)
        return pltpu.make_async_copy(turned_hbm.at[:, where, :], turned_ref.at[slot], reads.at[slot])

    def five(x, slot, wanted):
        sides = [three[pl.ds(x // 2 * 2 * channels + x % 2 * cols * chans, cols * chans)]]
        if wanted == 2:
            sides.append(three[pl.ds(x // 2 * 2 * channels + cols * chans, cols * chans)])
        sides = [side.reshape(depth, lanes) for side in sides]
        side = sides[0] if wanted == 1 else jnp.concatenate(sides, axis=1)
        part = dot(turned_ref[slot].reshape(group, depth), side)
        for j in range(wanted):
            where = pl.ds(pl.multiple_of((x + j) * group, group), group)
            for h in range(lanes // LANES):
                begin = j * lanes + h * LANES
                wide[h, where, :] = part[:, begin : begin + LANES]

    read(0).start()
    read(0).wait()
    lax.fori_loop(0, pairs + LAG + 1, trade, 0)

    span = 2 * (channels - cols * chans)

    def spot(index):
        return index // span * 2 * channels + 2 * cols * chans + index % span

    def made(owner, piece):
        return three.at[spot(piece * blocks + owner)]

    def come(place, piece):
        return three.at[spot((pieces + piece) * blocks + place)]

    def give(piece, slot, row, owner, place):
        sems = gave.at[slot, piece], took.at[place, piece]
        return remote(made(owner, piece), come(place, piece), *sems, {"row": row})

    def taken(piece, place):
        target = come(place, piece)
        return remote(target, target, gave.at[0, piece], took.at[place, piece], {"row": me})

    def hand(piece):
        for r, hands in SCATTER_HANDS.items():

            @pl.when(me == r)
            def _(r=r, hands=hands):
                for i, (row, owner, place, origin) in enumerate(hands):
                    taken(piece, origin).wait_recv()
                    value = made(owner, piece)[...].astype(jnp.float32)
                    value = value + come(origin, piece)[...].astype(jnp.float32)
                    made(owner, piece)[...] = value.astype(jnp.bfloat16)
                    give(piece, len(SCATTER_SENDS[r]) + i, row, owner, place).start()

    def settle(piece, carry):
        for r, origins in SCATTER_FROM.items():

            @pl.when(me == r)
            def _(r=r, origins=origins):
                for place in origins:
                    taken(piece, place).wait_recv()
                value = made(r, piece)[...].astype(jnp.float32)
                for place in origins:
                    value = value + come(place, piece)[...].astype(jnp.float32)
                out_ref[at(piece), :] = value.astype(jnp.bfloat16)

        return carry

    def pick(piece):
        wide_lanes = pairs * lanes // pieces
        span = LANES * pairs // wide_lanes
        where = pl.ds(pl.multiple_of(piece // span * LANES, LANES), LANES)
        side = jnp.concatenate([full(x, col, chan)[:, where] for x in range(pairs)], axis=1)
        shape = (pairs * LANES, wide_lanes)
        source = lax.broadcasted_iota(jnp.int32, shape, 0)
        target = lax.broadcasted_iota(jnp.int32, shape, 1) + piece % span * wide_lanes
        wanted = target % pairs * LANES + target // pairs
        chosen = jnp.where(source == wanted, 1.0, 0.0).astype(jnp.bfloat16)
        lands = pl.ds(pl.multiple_of(piece * wide_lanes, wide_lanes), wide_lanes)
        kept_ref[:, lands] = dot(side, chosen).astype(jnp.bfloat16)

    def reverse(piece, carry):
        now = lax.rem(piece, 2)

        @pl.when(piece > 0)
        def _():
            read(piece).wait()

        @pl.when(piece + 1 < pieces)
        def _():
            read(piece + 1).start()

        @pl.when(piece > 0)
        def _():
            def step_five(p, carry):
                five(2 * p, now, 2)
                return carry

            lax.fori_loop(0, pairs // 2, step_five, 0, unroll=2)

        def six(b, carry):
            sides = []
            for j in range(2):
                where = pl.ds(2 * b + j, channels * pairs, stride=tile)
                for h in range(lanes // LANES):
                    sides.append(wide.at[h][where, :].astype(jnp.bfloat16))
            part = dot(mpo_ref[...], jnp.concatenate(sides, axis=1)).astype(jnp.bfloat16)
            for j in range(2):
                where = pl.ds(pl.multiple_of((2 * b + j) * pairs, pairs), pairs)
                half = part[:, j * lanes : (j + 1) * lanes]
                for w in range(channels):
                    lhs[where, w * lanes : (w + 1) * lanes] = half[w * pairs : (w + 1) * pairs]
            return carry

        lax.fori_loop(0, tile // 2, six, 0, unroll=4)

        for r in range(0, blocks, 2):
            part = dot(lhs[...], left_ref[:, r * width : (r + 2) * width]).astype(jnp.bfloat16)
            made(r, piece)[...] = part[:, :width]
            made(r + 1, piece)[...] = part[:, width:]

        @pl.when(piece == 0)
        def _():
            pl.semaphore_wait(clear, blocks - 1)

        for r, sends in SCATTER_SENDS.items():

            @pl.when(me == r)
            def _(r=r, sends=sends):
                for slot, item in enumerate(sends):
                    give(piece, slot, *item).start()

        @pl.when(piece >= LATE)
        def _():
            hand(piece - LATE)

        pick(piece)
        return carry

    lax.fori_loop(0, pieces, reverse, 0)

    def late(piece, carry):
        hand(piece)
        return carry

    lax.fori_loop(pieces - LATE, pieces, late, 0)

    lax.fori_loop(0, pieces, settle, 0)
    for r, sends in SCATTER_SENDS.items():

        @pl.when(me == r)
        def _(r=r, sends=sends):
            def drain(piece, carry):
                hands = tuple(item[:3] for item in SCATTER_HANDS.get(r, ()))
                for slot, item in enumerate(sends + hands):
                    give(piece, slot, *item).wait_send()
                return carry

            lax.fori_loop(0, pieces, drain, 0)

    def finish(x, carry):
        @pl.when(x >= pairs - slots)
        def _():
            to_core(x).wait_send()

        to_chip(x).wait_send()
        for item in back(x):
            item.wait_send()
        return carry

    lax.fori_loop(0, pairs, finish, 0)


def fused(theta, left, first, second, right, pairs, tile):
    steps, width = theta.shape
    channels, rows, bonds = right.shape
    depth, lanes = left.shape[1], width
    pieces = bonds // tile
    cols, chans = lax.axis_size("col"), lax.axis_size("chan")
    own = rows // (cols * chans)
    flops = 4 * steps * left.size + 4 * bonds * (channels * pairs) ** 2 * lanes
    flops += 4 * right.size * pairs * lanes
    size = 2 * (2 * theta.size + left.size + 3 * right.size) + 2 * own * pairs * lanes
    far = pl.BlockSpec(memory_space=pl.ANY)
    near = pl.BlockSpec(memory_space=pltpu.VMEM)
    return pl.pallas_call(
        functools.partial(kernel, pieces),
        out_shape=[
            jax.ShapeDtypeStruct((steps, width), jnp.bfloat16),
            jax.ShapeDtypeStruct((own, pairs * lanes), jnp.bfloat16),
            jax.ShapeDtypeStruct((channels, bonds, rows), jnp.bfloat16),
        ],
        in_specs=[far, far, near, near, far],
        out_specs=[near, near, far],
        scratch_shapes=[
            pltpu.VMEM((steps, depth), jnp.bfloat16),
            pltpu.VMEM(left.shape, jnp.bfloat16),
            pltpu.VMEM((rows, channels * bonds), jnp.bfloat16),
            pltpu.VMEM((tile, channels, pairs, lanes), jnp.bfloat16),
            pltpu.VMEM((lanes // LANES, channels * pairs * tile, LANES), jnp.float32),
            pltpu.VMEM((channels * pairs, bonds, lanes), jnp.bfloat16),
            pltpu.VMEM((SLOTS, cols, own, chans * lanes), jnp.bfloat16),
            pltpu.VMEM((2, channels, tile, rows), jnp.bfloat16),
            pltpu.VMEM((tile * pairs, channels * lanes), jnp.bfloat16),
            pltpu.VMEM((channels * pairs, channels * pairs), jnp.bfloat16),
            pltpu.VMEM((channels * pairs, channels * pairs), jnp.bfloat16),
            pltpu.SemaphoreType.DMA((4, pieces)),
            pltpu.SemaphoreType.DMA((4, pieces)),
            pltpu.SemaphoreType.DMA((2 + channels,)),
            pltpu.SemaphoreType.DMA((2,)),
            pltpu.SemaphoreType.DMA((2, pairs)),
            pltpu.SemaphoreType.DMA((2, pairs)),
            pltpu.SemaphoreType.DMA((chans, pairs)),
            pltpu.SemaphoreType.DMA((chans, pairs)),
            pltpu.SemaphoreType.DMA((chans, pairs)),
            pltpu.SemaphoreType.REGULAR((2,)),
            pltpu.SemaphoreType.DMA((4, pieces)),
            pltpu.SemaphoreType.DMA((4, pieces)),
            pltpu.SemaphoreType.REGULAR,
            pltpu.SemaphoreType.DMA((2,)),
        ],
        compiler_params=pltpu.CompilerParams(
            collective_id=1, has_side_effects=True, vmem_limit_bytes=LIMIT
        ),
        cost_estimate=cost(flops, size),
    )(theta, left, first, second, right)


def mpo_product(mpo_left, mpo_right):
    paired = jnp.einsum("wuxs,uvyt->wstxyv", mpo_left, mpo_right, precision=lax.Precision.HIGHEST)
    channels, phys = mpo_left.shape[0], mpo_left.shape[2]
    return paired.reshape(channels * phys * phys, phys * phys * channels).astype(jnp.bfloat16)


def tiled_shards(theta, left_env, right_env, mpo_left, mpo_right):
    lanes, channels, depth = left_env.shape
    pairs, bonds = theta.shape[1:]
    width = theta.shape[0]
    tile = 16

    turned = jnp.transpose(theta, (2, 1, 0)).reshape(bonds * pairs, width)
    first = jnp.transpose(mpo_left, (0, 2, 3, 1)).reshape(channels * pairs, channels)
    second = jnp.transpose(mpo_right, (0, 2, 3, 1)).reshape(channels * pairs, channels)
    left = jnp.transpose(left_env, (1, 0, 2)).reshape(channels * lanes, depth)
    right = jnp.transpose(right_env, (1, 0, 2))

    product, residual, _ = fused(turned, left, first, second, right, pairs, tile)
    return residual, jnp.transpose(product.reshape(bonds, pairs, width), (2, 1, 0))


def plain_shards(theta, left_env, right_env, mpo_left, mpo_right):
    left_rows, channels = left_env.shape[:2]
    pairs, right_rows = theta.shape[1:]
    mpo_pair = mpo_product(mpo_left, mpo_right)
    einsum = functools.partial(jnp.einsum, preferred_element_type=jnp.float32)
    one = einsum("awk,ksb->awsb", left_env, lax.all_gather(theta, "row", axis=0, tiled=True))
    one = one.astype(jnp.bfloat16).reshape(left_rows, channels * pairs, right_rows)
    three = einsum("pq,apb->aqb", mpo_pair, one).astype(jnp.bfloat16)
    three = three.reshape(left_rows, pairs, channels, right_rows)
    term = einsum("kvb,asvb->kas", right_env, three).astype(jnp.bfloat16)
    term = term.reshape(right_env.shape[0], left_rows * pairs)
    residual = lax.psum_scatter(term, ("col", "chan"), scatter_dimension=0, tiled=True)
    full = lax.all_gather(residual, ("col", "chan"), axis=0, tiled=True)
    back = einsum("kp,kvb->pvb", full, right_env).astype(jnp.bfloat16)
    back = back.reshape(left_rows, pairs * channels, right_rows)
    back = einsum("pq,aqb->apb", mpo_pair, back).astype(jnp.bfloat16)
    back = back.reshape(left_rows, channels, pairs, right_rows)
    product = einsum("awk,awsb->ksb", left_env, back).astype(jnp.bfloat16)
    return residual, lax.psum_scatter(product, "row", scatter_dimension=0, tiled=True)


def shards(theta, left_env, right_env, mpo_left, mpo_right):
    sizes = [lax.axis_size(name) for name in ("row", "col", "chan")]
    fits = sizes == [4, 2, 2] and theta.shape == (256, 16, 256)
    fits = fits and left_env.shape == (256, 12, 1024) and right_env.shape == (1024, 12, 256)
    body = tiled_shards if fits else plain_shards
    return body(theta, left_env, right_env, mpo_left, mpo_right)


def solution(mesh):
    in_specs = (
        P(("grp", "row"), None, ("col", "chan")),
        P(("grp", "row"), None, None),
        P("grp", None, ("col", "chan")),
        P(),
        P(),
    )
    out_specs = (P(("grp", "col", "chan"), "row"), P(("grp", "row"), None, ("col", "chan")))
    return jax.shard_map(shards, mesh=mesh, in_specs=in_specs, out_specs=out_specs, check_vma=False)
```

```python
import functools
import math

import jax
import jax.numpy as jnp
from jax import lax
from jax.experimental import pallas as pl
from jax.experimental.pallas import tpu as pltpu
from jax.sharding import PartitionSpec as P

LANES = 128
AHEAD = 3
SLOTS = 4
LAG = 4
LATE = 1
LIMIT = 61 * 1024 * 1024
MESH = pl.DeviceIdType.MESH


def cost(flops, size):
    return pl.CostEstimate(flops=int(flops), bytes_accessed=int(size), transcendentals=0)


def dot(lhs, rhs):
    return jnp.dot(lhs, rhs, preferred_element_type=jnp.float32)


def greet(peers):
    barrier = pltpu.get_barrier_semaphore()
    for peer in peers:
        pl.semaphore_signal(barrier, inc=1, device_id=peer, device_id_type=MESH)
    pl.semaphore_wait(barrier, len(peers))


def row_peers():
    size = lax.axis_size("row")
    return [{"row": lax.rem(lax.axis_index("row") + step, size)} for step in range(1, size)]


def remote(source, target, send_sem, recv_sem, peer):
    return pltpu.make_async_remote_copy(
        src_ref=source,
        dst_ref=target,
        send_sem=send_sem,
        recv_sem=recv_sem,
        device_id=peer,
        device_id_type=MESH,
    )


def pair_product(first_ref, second_ref, front_ref, mpo_ref, channels):
    size = mpo_ref.shape[0]
    phys = math.isqrt(size // channels)

    def exact(lhs, rhs, dims=(((1,), (0,)), ((), ()))):
        return lax.dot_general(
            lhs, rhs, dims, precision=lax.Precision.HIGHEST, preferred_element_type=jnp.float32
        )

    def ones(wanted):
        return jnp.where(wanted, 1.0, 0.0).astype(jnp.float32)

    row = lax.broadcasted_iota(jnp.int32, (size, size), 0)
    lane = lax.broadcasted_iota(jnp.int32, (size, size), 1)
    shape = (channels, size)
    own = lax.broadcasted_iota(jnp.int32, shape, 0)
    other = lax.broadcasted_iota(jnp.int32, shape, 1)
    second = exact(second_ref[...], ones(other % channels == own))
    second = jnp.where(lane // channels == row % (phys * phys), second, 0.0)
    second = exact(ones(other // (phys * phys) == own), second)
    both = exact(first_ref[...], second)
    total = jnp.zeros((size, size), jnp.float32)
    for x in range(phys):
        source = row // (phys * phys) * (phys * phys) + x * phys + row // phys % phys
        part = exact(ones(lane == source), both)
        part = jnp.where(lane // channels % phys == row % phys, part, 0.0)
        target = (x * phys + row // (phys * channels)) * channels + row % channels
        total = total + exact(part, ones(lane == target))
    mpo_ref[...] = total.astype(jnp.bfloat16)
    turned = exact(ones(lane == row), total, (((1,), (1,)), ((), ())))
    front_ref[...] = turned.astype(jnp.bfloat16)


GATHER_SENDS = {0: (1, 2), 1: (2, 0, 3), 2: (1, 3, 0), 3: (2, 1)}
GATHER_HANDS = {1: (3, 0), 2: (0, 3)}


SCATTER_SENDS = {
    0: ((1, 3, 1), (1, 2, 3), (1, 1, 0)),
    1: ((0, 0, 1),),
    2: ((3, 3, 2),),
    3: ((2, 0, 2), (2, 1, 0), (2, 2, 3)),
}
SCATTER_HANDS = {1: ((3, 3, 1, 1), (2, 2, 1, 3)), 2: ((0, 0, 2, 2), (1, 1, 2, 0))}
SCATTER_FROM = {0: (1, 2), 1: (0, 2), 2: (3, 1), 3: (2, 1)}


def kernel(
    pieces, theta_ref, left_hbm, first_ref, second_ref, right_hbm, out_hbm, kept_hbm, turned_hbm,
    gathered, left_ref, right_ref, held, wide, three, terms, turned_ref, lhs, front_ref, mpo_ref,
    out_ref, kept_ref, sent, got, local, turns, swap_sent, swap_got, full_sent, full_got, keeps, free,
    gave, took, clear, reads, ends,
):
    width = theta_ref.shape[1]
    tile, channels, pairs, lanes = held.shape
    _, bonds, _ = three.shape
    slots, cols, rows, lump = terms.shape
    chans = lump // lanes
    depth = cols * chans * rows
    blocks = gathered.shape[1] // width
    step = tile * pairs
    group = channels * tile
    me, col, chan = lax.axis_index("row"), lax.axis_index("col"), lax.axis_index("chan")
    core, chip = {"col": 1 - col}, {"chan": 1 - chan}
    loads = [
        pltpu.make_async_copy(
            right_hbm.at[v], right_ref.at[:, v * bonds : (v + 1) * bonds], local.at[2 + v]
        )
        for v in range(channels)
    ]
    loads.append(pltpu.make_async_copy(left_hbm, left_ref, local.at[0]))
    for item in loads:
        item.start()

    def at(piece):
        return pl.ds(pl.multiple_of(piece * step, step), step)

    def block(piece, origin):
        return gathered.at[at(piece), origin * width : (origin + 1) * width]

    def send(piece, origin, slot, row, source=None):
        source = theta_ref.at[at(piece), :] if source is None else source
        return remote(
            source, block(piece, origin), sent.at[slot, piece], got.at[origin, piece], {"row": row}
        )

    def arrival(piece, origin):
        return send(piece, origin, 0, me)

    greet(row_peers() + [core, chip])
    for r, rows_to in GATHER_SENDS.items():

        @pl.when(me == r)
        def _(r=r, rows_to=rows_to):
            for piece in range(min(AHEAD, pieces)):
                for slot, row in enumerate(rows_to):
                    send(piece, r, slot, row).start()
            mine = pltpu.make_async_copy(
                theta_ref, gathered.at[:, r * width : (r + 1) * width], local.at[1]
            )
            mine.start()
            mine.wait()

    pair_product(first_ref, second_ref, front_ref, mpo_ref, channels)
    for item in loads:
        item.wait()

    def stage(slot):
        return lhs.at[:, pl.ds(pl.multiple_of(slot * depth, depth), depth)]

    def turned(v):
        slot = lax.rem(v, 2)
        return pltpu.make_async_copy(stage(slot), turned_hbm.at[v], turns.at[slot])

    def turn(v, carry):
        @pl.when(v >= 2)
        def _():
            turned(v - 2).wait()

        where = pl.ds(pl.multiple_of(v * bonds, bonds), bonds)
        stage(lax.rem(v, 2))[...] = right_ref[:, where].T
        turned(v).start()
        return carry

    lax.fori_loop(0, channels, turn, 0)
    for v in range(channels - 2, channels):
        turned(v).wait()

    def body(piece, carry):
        for r, rows_to in GATHER_SENDS.items():

            @pl.when(me == r)
            def _(r=r, rows_to=rows_to):
                late = [origin for origin in range(4) if origin != r]
                if r in GATHER_HANDS:
                    origin, row = GATHER_HANDS[r]
                    arrival(piece, origin).wait_recv()
                    send(piece, origin, len(rows_to), row, block(piece, origin)).start()
                    late.remove(origin)
                for origin in late:
                    arrival(piece, origin).wait_recv()

                @pl.when(piece + AHEAD < pieces)
                def _():
                    for slot, row in enumerate(rows_to):
                        send(piece + AHEAD, r, slot, row).start()

        def one(w, carry):
            where = pl.ds(pl.multiple_of(2 * w * lanes, 2 * lanes), 2 * lanes)
            part = lax.dot_general(
                gathered[at(piece), :],
                left_ref[where, :],
                (((1,), (1,)), ((), ())),
                preferred_element_type=jnp.float32,
            ).astype(jnp.bfloat16)
            held[:, 2 * w] = part[:, :lanes].reshape(tile, pairs, lanes)
            held[:, 2 * w + 1] = part[:, lanes:].reshape(tile, pairs, lanes)
            return carry

        lax.fori_loop(0, channels // 2, one, 0, unroll=3)

        def two(b, carry):
            first = held[2 * b].reshape(channels * pairs, lanes)
            second = held[2 * b + 1].reshape(channels * pairs, lanes)
            part = dot(front_ref[...], jnp.concatenate([first, second], axis=1))
            for j in range(2):
                where = pl.ds(2 * b + j, channels * pairs, stride=tile)
                for h in range(lanes // LANES):
                    begin = j * lanes + h * LANES
                    wide.at[h][where, :] = part[:, begin : begin + LANES]
            return carry

        lax.fori_loop(0, tile // 2, two, 0, unroll=8)

        def pack(x, carry):
            own = pl.ds(pl.multiple_of(x * group, group), group)
            where = pl.ds(pl.multiple_of(piece * tile, tile), tile)
            for h in range(lanes // LANES):
                part = wide[h, own, :].astype(jnp.bfloat16).reshape(channels, tile, LANES)
                three[pl.ds(x * channels, channels), where, h * LANES : (h + 1) * LANES] = part
            return carry

        lax.fori_loop(0, pairs, pack, 0, unroll=4)
        return carry

    lax.fori_loop(0, pieces, body, 0)
    for r, rows_to in GATHER_SENDS.items():

        @pl.when(me == r)
        def _(r=r, rows_to=rows_to):
            def finish(piece, carry):
                for slot, row in enumerate(rows_to):
                    send(piece, r, slot, row).wait_send()
                if r in GATHER_HANDS:
                    origin, row = GATHER_HANDS[r]
                    send(piece, origin, len(rows_to), row, block(piece, origin)).wait_send()
                return carry

            lax.fori_loop(0, pieces, finish, 0)

    pl.semaphore_signal(free.at[0], inc=1, device_id=core, device_id_type=MESH)
    pl.semaphore_signal(free.at[1], inc=1, device_id=chip, device_id_type=MESH)

    def near(x, first=0):
        where = pl.ds(pl.multiple_of((first + x // 2) * rows, rows), rows)
        return gathered.at[where, pl.ds(pl.multiple_of(x % 2 * lump, lump), lump)]

    def far(x):
        return near(x, pairs // 2)

    def to_core(x):
        source = terms.at[lax.rem(x, slots), 1 - col]
        return remote(source, near(x), swap_sent.at[0, x], swap_got.at[0, x], core)

    def to_chip(x):
        return remote(near(x), far(x), swap_sent.at[1, x], swap_got.at[1, x], chip)

    def full(x, c, d):
        return three.at[x // 2 * 2 * channels + x % 2 * cols * chans + c * chans + d]

    def places(x):
        for d in range(chans):
            where = pl.ds(pl.multiple_of((x // 2 + pairs // 2) * rows, rows), rows)
            begin = pl.multiple_of(x % 2 * lump + d * lanes, lanes)
            yield d, gathered.at[where, pl.ds(begin, lanes)], full(x, col, d)

    def back(x):
        return [
            remote(source, target, full_sent.at[d, x], full_got.at[d, x], core)
            for d, source, target in places(x)
        ]

    def keep(x):
        return [
            pltpu.make_async_copy(source, target, keeps.at[d, x]) for d, source, target in places(x)
        ]

    def term(x):
        side = three[pl.ds(x * channels, channels)].reshape(channels * bonds, lanes)
        value = dot(right_ref[...], side).astype(jnp.bfloat16)
        for c in range(cols):
            for d in range(chans):
                part = value[(c * chans + d) * rows : (c * chans + d + 1) * rows]
                terms[lax.rem(x, slots), c, :, d * lanes : (d + 1) * lanes] = part

    def join(x):
        to_core(x).wait_recv()
        value = near(x)[...].astype(jnp.float32)
        value = value + terms[lax.rem(x, slots), col].astype(jnp.float32)
        near(x)[...] = value.astype(jnp.bfloat16)

        @pl.when(x == 0)
        def _():
            pl.semaphore_wait(free.at[1], 1)

        to_chip(x).start()

    def close(x):
        to_chip(x).wait_recv()
        value = near(x)[...].astype(jnp.float32) + far(x)[...].astype(jnp.float32)
        far(x)[...] = value.astype(jnp.bfloat16)
        for item in back(x) + keep(x):
            item.start()

    def trade(x, carry):
        @pl.when(x < pairs)
        def _():
            @pl.when(x >= slots)
            def _():
                to_core(x - slots).wait_send()

            term(x)

            @pl.when(x == 0)
            def _():
                pl.semaphore_wait(free.at[0], 1)

            to_core(x).start()

        @pl.when((x >= 1) & (x <= pairs))
        def _():
            join(x - 1)

        @pl.when((x >= LAG) & (x < pairs + LAG))
        def _():
            close(x - LAG)

        @pl.when(x >= LAG + 1)
        def _():
            for item in back(x - LAG - 1):
                item.wait_recv()
            for item in keep(x - LAG - 1):
                item.wait()
            five(x - LAG - 1, 0, 1)

        @pl.when(x == pairs)
        def _():
            for peer in row_peers():
                pl.semaphore_signal(clear, inc=1, device_id=peer, device_id_type=MESH)

        return carry

    def read(piece):
        where = pl.ds(pl.multiple_of(piece * tile, tile), tile)
        slot = lax.rem(piece, 2)
        return pltpu.make_async_copy(turned_hbm.at[:, where, :], turned_ref.at[slot], reads.at[slot])

    def five(x, slot, wanted):
        sides = [three[pl.ds(x // 2 * 2 * channels + x % 2 * cols * chans, cols * chans)]]
        if wanted == 2:
            sides.append(three[pl.ds(x // 2 * 2 * channels + cols * chans, cols * chans)])
        sides = [side.reshape(depth, lanes) for side in sides]
        side = sides[0] if wanted == 1 else jnp.concatenate(sides, axis=1)
        part = dot(turned_ref[slot].reshape(group, depth), side)
        for j in range(wanted):
            where = pl.ds(pl.multiple_of((x + j) * group, group), group)
            for h in range(lanes // LANES):
                begin = j * lanes + h * LANES
                wide[h, where, :] = part[:, begin : begin + LANES]

    read(0).start()
    read(0).wait()
    lax.fori_loop(0, pairs + LAG + 1, trade, 0)

    span = 2 * (channels - cols * chans)

    def spot(index):
        return index // span * 2 * channels + 2 * cols * chans + index % span

    def made(owner, piece):
        return three.at[spot(piece * blocks + owner)]

    def come(place, piece):
        return three.at[spot((pieces + piece) * blocks + place)]

    def give(piece, slot, row, owner, place):
        sems = gave.at[slot, piece], took.at[place, piece]
        return remote(made(owner, piece), come(place, piece), *sems, {"row": row})

    def taken(piece, place):
        target = come(place, piece)
        return remote(target, target, gave.at[0, piece], took.at[place, piece], {"row": me})

    def hand(piece):
        for r, hands in SCATTER_HANDS.items():

            @pl.when(me == r)
            def _(r=r, hands=hands):
                for i, (row, owner, place, origin) in enumerate(hands):
                    taken(piece, origin).wait_recv()
                    value = made(owner, piece)[...].astype(jnp.float32)
                    value = value + come(origin, piece)[...].astype(jnp.float32)
                    made(owner, piece)[...] = value.astype(jnp.bfloat16)
                    give(piece, len(SCATTER_SENDS[r]) + i, row, owner, place).start()

    def leave(piece):
        return pltpu.make_async_copy(
            out_ref.at[at(piece), :], out_hbm.at[at(piece), :], ends.at[piece]
        )

    def settle(piece, carry):
        for r, origins in SCATTER_FROM.items():

            @pl.when(me == r)
            def _(r=r, origins=origins):
                for place in origins:
                    taken(piece, place).wait_recv()
                value = made(r, piece)[...].astype(jnp.float32)
                for place in origins:
                    value = value + come(place, piece)[...].astype(jnp.float32)
                out_ref[at(piece), :] = value.astype(jnp.bfloat16)

        leave(piece).start()
        return carry

    def pick(piece):
        wide_lanes = pairs * lanes // pieces
        span = LANES * pairs // wide_lanes
        where = pl.ds(pl.multiple_of(piece // span * LANES, LANES), LANES)
        side = jnp.concatenate([full(x, col, chan)[:, where] for x in range(pairs)], axis=1)
        shape = (pairs * LANES, wide_lanes)
        source = lax.broadcasted_iota(jnp.int32, shape, 0)
        target = lax.broadcasted_iota(jnp.int32, shape, 1) + piece % span * wide_lanes
        wanted = target % pairs * LANES + target // pairs
        chosen = jnp.where(source == wanted, 1.0, 0.0).astype(jnp.bfloat16)
        lands = pl.ds(pl.multiple_of(piece * wide_lanes, wide_lanes), wide_lanes)
        kept_ref[:, lands] = dot(side, chosen).astype(jnp.bfloat16)

    def reverse(piece, carry):
        now = lax.rem(piece, 2)

        @pl.when(piece > 0)
        def _():
            read(piece).wait()

        @pl.when(piece + 1 < pieces)
        def _():
            read(piece + 1).start()

        @pl.when(piece > 0)
        def _():
            def step_five(p, carry):
                five(2 * p, now, 2)
                return carry

            lax.fori_loop(0, pairs // 2, step_five, 0, unroll=2)

        def six(b, carry):
            sides = []
            for j in range(2):
                where = pl.ds(2 * b + j, channels * pairs, stride=tile)
                for h in range(lanes // LANES):
                    sides.append(wide.at[h][where, :].astype(jnp.bfloat16))
            part = dot(mpo_ref[...], jnp.concatenate(sides, axis=1)).astype(jnp.bfloat16)
            for j in range(2):
                where = pl.ds(pl.multiple_of((2 * b + j) * pairs, pairs), pairs)
                half = part[:, j * lanes : (j + 1) * lanes]
                for w in range(channels):
                    lhs[where, w * lanes : (w + 1) * lanes] = half[w * pairs : (w + 1) * pairs]
            return carry

        lax.fori_loop(0, tile // 2, six, 0, unroll=8)

        for r in range(0, blocks, 2):
            part = dot(lhs[...], left_ref[:, r * width : (r + 2) * width]).astype(jnp.bfloat16)
            made(r, piece)[...] = part[:, :width]
            made(r + 1, piece)[...] = part[:, width:]

        @pl.when(piece == 0)
        def _():
            pl.semaphore_wait(clear, blocks - 1)

        for r, sends in SCATTER_SENDS.items():

            @pl.when(me == r)
            def _(r=r, sends=sends):
                for slot, item in enumerate(sends):
                    give(piece, slot, *item).start()

        @pl.when(piece >= LATE)
        def _():
            hand(piece - LATE)

        pick(piece)
        return carry

    lax.fori_loop(0, pieces, reverse, 0)
    kept = pltpu.make_async_copy(kept_ref, kept_hbm, ends.at[pieces])
    kept.start()

    def late(piece, carry):
        hand(piece)
        return carry

    lax.fori_loop(pieces - LATE, pieces, late, 0)

    lax.fori_loop(0, pieces, settle, 0)
    for r, sends in SCATTER_SENDS.items():

        @pl.when(me == r)
        def _(r=r, sends=sends):
            def drain(piece, carry):
                hands = tuple(item[:3] for item in SCATTER_HANDS.get(r, ()))
                for slot, item in enumerate(sends + hands):
                    give(piece, slot, *item).wait_send()
                return carry

            lax.fori_loop(0, pieces, drain, 0)

    def finish(x, carry):
        @pl.when(x >= pairs - slots)
        def _():
            to_core(x).wait_send()

        to_chip(x).wait_send()
        for item in back(x):
            item.wait_send()
        return carry

    lax.fori_loop(0, pairs, finish, 0)

    def done(piece, carry):
        leave(piece).wait()
        return carry

    lax.fori_loop(0, pieces, done, 0)
    kept.wait()


def fused(theta, left, first, second, right, pairs, tile):
    steps, width = theta.shape
    channels, rows, bonds = right.shape
    depth, lanes = left.shape[1], width
    pieces = bonds // tile
    cols, chans = lax.axis_size("col"), lax.axis_size("chan")
    own = rows // (cols * chans)
    flops = 4 * steps * left.size + 4 * bonds * (channels * pairs) ** 2 * lanes
    flops += 4 * right.size * pairs * lanes
    size = 2 * (2 * theta.size + left.size + 3 * right.size) + 2 * own * pairs * lanes
    far = pl.BlockSpec(memory_space=pl.ANY)
    near = pl.BlockSpec(memory_space=pltpu.VMEM)
    return pl.pallas_call(
        functools.partial(kernel, pieces),
        out_shape=[
            jax.ShapeDtypeStruct((steps, width), jnp.bfloat16),
            jax.ShapeDtypeStruct((own, pairs * lanes), jnp.bfloat16),
            jax.ShapeDtypeStruct((channels, bonds, rows), jnp.bfloat16),
        ],
        in_specs=[far, far, near, near, far],
        out_specs=[far, far, far],
        scratch_shapes=[
            pltpu.VMEM((steps, depth), jnp.bfloat16),
            pltpu.VMEM(left.shape, jnp.bfloat16),
            pltpu.VMEM((rows, channels * bonds), jnp.bfloat16),
            pltpu.VMEM((tile, channels, pairs, lanes), jnp.bfloat16),
            pltpu.VMEM((lanes // LANES, channels * pairs * tile, LANES), jnp.float32),
            pltpu.VMEM((channels * pairs, bonds, lanes), jnp.bfloat16),
            pltpu.VMEM((SLOTS, cols, own, chans * lanes), jnp.bfloat16),
            pltpu.VMEM((2, channels, tile, rows), jnp.bfloat16),
            pltpu.VMEM((tile * pairs, channels * lanes), jnp.bfloat16),
            pltpu.VMEM((channels * pairs, channels * pairs), jnp.bfloat16),
            pltpu.VMEM((channels * pairs, channels * pairs), jnp.bfloat16),
            pltpu.VMEM((steps, width), jnp.bfloat16),
            pltpu.VMEM((own, pairs * lanes), jnp.bfloat16),
            pltpu.SemaphoreType.DMA((4, pieces)),
            pltpu.SemaphoreType.DMA((4, pieces)),
            pltpu.SemaphoreType.DMA((2 + channels,)),
            pltpu.SemaphoreType.DMA((2,)),
            pltpu.SemaphoreType.DMA((2, pairs)),
            pltpu.SemaphoreType.DMA((2, pairs)),
            pltpu.SemaphoreType.DMA((chans, pairs)),
            pltpu.SemaphoreType.DMA((chans, pairs)),
            pltpu.SemaphoreType.DMA((chans, pairs)),
            pltpu.SemaphoreType.REGULAR((2,)),
            pltpu.SemaphoreType.DMA((4, pieces)),
            pltpu.SemaphoreType.DMA((4, pieces)),
            pltpu.SemaphoreType.REGULAR,
            pltpu.SemaphoreType.DMA((2,)),
            pltpu.SemaphoreType.DMA((pieces + 1,)),
        ],
        compiler_params=pltpu.CompilerParams(
            collective_id=1, has_side_effects=True, vmem_limit_bytes=LIMIT
        ),
        cost_estimate=cost(flops, size),
    )(theta, left, first, second, right)


def mpo_product(mpo_left, mpo_right):
    paired = jnp.einsum("wuxs,uvyt->wstxyv", mpo_left, mpo_right, precision=lax.Precision.HIGHEST)
    channels, phys = mpo_left.shape[0], mpo_left.shape[2]
    return paired.reshape(channels * phys * phys, phys * phys * channels).astype(jnp.bfloat16)


def tiled_shards(theta, left_env, right_env, mpo_left, mpo_right):
    lanes, channels, depth = left_env.shape
    pairs, bonds = theta.shape[1:]
    width = theta.shape[0]
    tile = 16

    turned = jnp.transpose(theta, (2, 1, 0)).reshape(bonds * pairs, width)
    first = jnp.transpose(mpo_left, (0, 2, 3, 1)).reshape(channels * pairs, channels)
    second = jnp.transpose(mpo_right, (0, 2, 3, 1)).reshape(channels * pairs, channels)
    left = jnp.transpose(left_env, (1, 0, 2)).reshape(channels * lanes, depth)
    right = jnp.transpose(right_env, (1, 0, 2))

    product, residual, _ = fused(turned, left, first, second, right, pairs, tile)
    return residual, jnp.transpose(product.reshape(bonds, pairs, width), (2, 1, 0))


def plain_shards(theta, left_env, right_env, mpo_left, mpo_right):
    left_rows, channels = left_env.shape[:2]
    pairs, right_rows = theta.shape[1:]
    mpo_pair = mpo_product(mpo_left, mpo_right)
    einsum = functools.partial(jnp.einsum, preferred_element_type=jnp.float32)
    one = einsum("awk,ksb->awsb", left_env, lax.all_gather(theta, "row", axis=0, tiled=True))
    one = one.astype(jnp.bfloat16).reshape(left_rows, channels * pairs, right_rows)
    three = einsum("pq,apb->aqb", mpo_pair, one).astype(jnp.bfloat16)
    three = three.reshape(left_rows, pairs, channels, right_rows)
    term = einsum("kvb,asvb->kas", right_env, three).astype(jnp.bfloat16)
    term = term.reshape(right_env.shape[0], left_rows * pairs)
    residual = lax.psum_scatter(term, ("col", "chan"), scatter_dimension=0, tiled=True)
    full = lax.all_gather(residual, ("col", "chan"), axis=0, tiled=True)
    back = einsum("kp,kvb->pvb", full, right_env).astype(jnp.bfloat16)
    back = back.reshape(left_rows, pairs * channels, right_rows)
    back = einsum("pq,aqb->apb", mpo_pair, back).astype(jnp.bfloat16)
    back = back.reshape(left_rows, channels, pairs, right_rows)
    product = einsum("awk,awsb->ksb", left_env, back).astype(jnp.bfloat16)
    return residual, lax.psum_scatter(product, "row", scatter_dimension=0, tiled=True)


def shards(theta, left_env, right_env, mpo_left, mpo_right):
    sizes = [lax.axis_size(name) for name in ("row", "col", "chan")]
    fits = sizes == [4, 2, 2] and theta.shape == (256, 16, 256)
    fits = fits and left_env.shape == (256, 12, 1024) and right_env.shape == (1024, 12, 256)
    body = tiled_shards if fits else plain_shards
    return body(theta, left_env, right_env, mpo_left, mpo_right)


def solution(mesh):
    in_specs = (
        P(("grp", "row"), None, ("col", "chan")),
        P(("grp", "row"), None, None),
        P("grp", None, ("col", "chan")),
        P(),
        P(),
    )
    out_specs = (P(("grp", "col", "chan"), "row"), P(("grp", "row"), None, ("col", "chan")))
    return jax.shard_map(shards, mesh=mesh, in_specs=in_specs, out_specs=out_specs, check_vma=False)
```
